32 devices in a mesh: seq: 4 (over y, x), batch: 8 (over z, core).
Axes of the slice: x: 2, y: 2, z: 4, core: 2. Of those that a mesh axis runs over, the one named last changes fastest.
Arguments:
- tokens: bfloat16 [8, 1024, 2048], P('batch', 'seq'), may hold values from -6 to 6
- cotangent: bfloat16 [8, 1024, 2048], P('batch', 'seq'), may hold values from -6 to 6
- segment_ids: int32 [8, 1024], P('batch'), may hold values from 0 to 3, never falling along the last dimension, each value on 1 to 512 neighbouring positions
- exit_mask: int32 [8, 8], P('batch', 'seq'), may hold values 0 or 1
- ln1_gain: bfloat16 [2048], P(('seq', 'batch')), may hold values from 0.099609375 to 1.8984375
- ln1_bias: bfloat16 [2048], P(('seq', 'batch')), may hold values from -3 to 3
- w_qkv: bfloat16 [2048, 6144], P(('seq', 'batch')), may hold values from -0.125 to 0.125
- b_qv: bfloat16 [4096], P(('seq', 'batch')), may hold values from -3 to 3
- w_out: bfloat16 [2048, 2048], P(('seq', 'batch')), may hold values from -2 to 2
- b_out: bfloat16 [2048], P(('seq', 'batch')), may hold values from -3 to 3
- ln2_gain: bfloat16 [2048], P(('seq', 'batch')), may hold values from 0.099609375 to 1.8984375
- ln2_bias: bfloat16 [2048], P(('seq', 'batch')), may hold values from -3 to 3
- w_up: bfloat16 [8192, 2048], P(('seq', 'batch')), may hold values from -0.125 to 0.125
- b_up: bfloat16 [8192], P(('seq', 'batch')), may hold values from -3 to 3
- w_down: bfloat16 [8192, 2048], P(('seq', 'batch')), may hold values from -0.09375 to 0.09375
- b_down: bfloat16 [2048], P(('seq', 'batch')), may hold values from -3 to 3
Outputs:
- layer_out: bfloat16 [8, 1024, 2048], P('batch', 'seq')
- input_grad: float32 [8, 1024, 2048], P('batch', 'seq')
- grad_ln1_gain: float32 [2048], P(('seq', 'batch'))
- grad_ln1_bias: float32 [2048], P(('seq', 'batch'))
- grad_w_qkv: float32 [2048, 6144], P(('seq', 'batch'))
- grad_b_qv: float32 [4096], P(('seq', 'batch'))
- grad_w_out: float32 [2048, 2048], P(('seq', 'batch'))
- grad_b_out: float32 [2048], P(('seq', 'batch'))
- grad_ln2_gain: float32 [2048], P(('seq', 'batch'))
- grad_ln2_bias: float32 [2048], P(('seq', 'batch'))
- grad_w_up: float32 [8192, 2048], P(('seq', 'batch'))
- grad_b_up: float32 [8192], P(('seq', 'batch'))
- grad_w_down: float32 [8192, 2048], P(('seq', 'batch'))
- grad_b_down: float32 [2048], P(('seq', 'batch'))
The draws below stay inside these ranges and needn't reach their ends.
All inputs are finite; a program needn't handle non-finite values. No bound on the sum of `exit_mask` on one device may be relied on, other than what follows from the above.
Results may differ from the reference program's by a relative error of at most 0.012.
Values may be sent and summed in bfloat16 or wider, within the bound.
No kernel may reach another device: no remote copies, remote signals or barrier semaphores. Data moves between devices by JAX's collectives and lax.ppermute only.
A program may use at most 512 MiB of HBM per device.

```python
import math
import jax
import jax.numpy as jnp
import numpy as np
from jax import lax

D = 2048
HEADS = 32
HEAD_DIM = 64
FF = 8192
TILE = 128
ROWS = 8
LEN = 1024


def plant(result, rng, low, high):
    place = [jax.random.randint(jax.random.fold_in(rng, axis), (), 0, length) for axis, length in enumerate(result.shape)]
    widest = result.shape.index(max(result.shape))
    neighbour = place[:widest] + [(place[widest] + 1) % result.shape[widest]] + place[widest + 1:]
    return result.at[tuple(place)].set(low).at[tuple(neighbour)].set(high)


def steps_of(rng, extent, split, least, high):
    def one(axis_at, blocks):
        draws = jax.random.uniform(jax.random.fold_in(jax.random.fold_in(rng, 6), axis_at), (blocks,), jnp.float32, least / len(split), high / len(split))
        return jnp.repeat(jnp.exp(draws), extent[axis_at] // blocks).reshape((-1,) + (1,) * (len(extent) - axis_at - 1))

    factor_of = one(*split[0])
    for cut in split[1:]:
        factor_of = factor_of * one(*cut)
    return factor_of


def length_profile(number_of, total, limit, lean):
    portions = [(1 << 20) // math.isqrt(rank ** lean) + 1 for rank in range(2, number_of + 1)]
    spare, given = total - limit - (number_of - 1), [1] * (number_of - 1)
    while spare > 0:
        candidates = [i for i in range(number_of - 1) if given[i] < limit]
        mass, left = sum([portions[i] for i in candidates]), spare
        for i in candidates:
            more = min(limit - given[i], max(1, left * portions[i] // mass), spare)
            given[i] = given[i] + more
            spare = spare - more
    return np.array([limit] + given)


def uneven_parts(rng, number_of, total, limit, lean):
    if number_of == 2:
        one = jax.random.randint(rng, (), max(1, total - limit), min(limit, total - 1) + 1)
        return jnp.stack([one, total - one])
    lengths = jnp.asarray(length_profile(number_of, total, limit, lean), jnp.int32)
    twos = (number_of - 1) // 2
    donor, receiver = lengths[1:1 + 2 * twos:2], lengths[2:2 + 2 * twos:2]
    margin = jnp.minimum(donor - 1, limit - receiver)
    moved = jax.random.randint(jax.random.fold_in(rng, 1), (twos,), 0, 1 << 20) % (margin + 1)
    lengths = lengths.at[1:1 + 2 * twos:2].set(donor - moved).at[2:2 + 2 * twos:2].set(receiver + moved)
    return lengths[jax.random.permutation(jax.random.fold_in(rng, 2), number_of)]


def gaussian(key, shape, deviation, limit, shards=(), kind=jnp.bfloat16):
    loudness = steps_of(key, shape, shards, -0.22, 0.18) if shards else 1.0
    result = jax.random.normal(key, shape, jnp.float32) * deviation * loudness
    return jnp.minimum(jnp.maximum(result, -limit), limit).astype(kind)


def setup_inputs(seed: int = 0) -> dict:
    key_of = jax.random.split(jax.random.key(seed), 17)
    return {
        "tokens": gaussian(key_of[0], (ROWS, LEN, D), 1.0, 6.0, ((0, 8), (1, 4))),
        "cotangent": gaussian(key_of[1], (ROWS, LEN, D), 1.0, 6.0, ((0, 8), (1, 4))),
        "segment_ids": jax.vmap(lambda own: jnp.searchsorted(jnp.cumsum(uneven_parts(own, 4, LEN, LEN // 2, 2)), jnp.arange(LEN), side="right"))(jax.random.split(key_of[2], ROWS)).reshape((ROWS, LEN)).astype(jnp.int32),
        "exit_mask": plant((jax.random.randint(key_of[3], (ROWS, LEN // TILE), 0, 4) < 3).astype(jnp.int32), jax.random.fold_in(key_of[3], 1), 0, 1),
        "ln1_gain": jnp.clip(1.0 + 0.18 * jax.random.normal(key_of[4], (D,), jnp.float32), 0.099609375, 1.8984375).astype(jnp.bfloat16),
        "ln1_bias": gaussian(key_of[5], (D,), 0.5, 3.0, ((0, 32),)),
        "w_qkv": gaussian(key_of[6], (D, 3 * D), D ** -0.5, 0.125, ((0, 32),)),
        "b_qv": gaussian(key_of[7], (2 * D,), 0.5, 3.0, ((0, 32),)),
        "w_out": gaussian(key_of[8], (D, D), (max(D // 256, 1)) ** -0.5, 2.0, ((0, 32),)),
        "b_out": gaussian(key_of[9], (D,), 0.5, 3.0, ((0, 32),)),
        "ln2_gain": jnp.clip(1.0 + 0.18 * jax.random.normal(key_of[10], (D,), jnp.float32), 0.099609375, 1.8984375).astype(jnp.bfloat16),
        "ln2_bias": gaussian(key_of[11], (D,), 0.5, 3.0, ((0, 32),)),
        "w_up": gaussian(key_of[12], (FF, D), D ** -0.5, 0.125, ((0, 32),)),
        "b_up": gaussian(key_of[13], (FF,), 0.5, 3.0, ((0, 32),)),
        "w_down": gaussian(key_of[14], (FF, D), (FF // 2) ** -0.5, 0.09375, ((0, 32),)),
        "b_down": gaussian(key_of[15], (D,), 0.5, 3.0, ((0, 32),)),
    }


@jax.custom_vjp
def low(v):
    return lax.optimization_barrier(v.astype(jnp.bfloat16)).astype(jnp.float32)

@jax.custom_vjp
def low_back(v):
    return v

def low_keep(v):
    return (low(v), None)

def low_pass(kept, grad):
    return (grad,)

def back_keep(v):
    return (v, None)

def back_low(kept, grad):
    return (low(grad),)
low.defvjp(low_keep, low_pass)
low_back.defvjp(back_keep, back_low)
EPSILON = 1e-05

def layer_norm(values, gain, shift):
    centre = lax.optimization_barrier(jnp.mean(values, axis=-1, keepdims=True))
    centred = values - centre
    spread = lax.optimization_barrier(jnp.mean(centred * centred, axis=-1, keepdims=True))
    return centred * lax.rsqrt(spread + EPSILON) * gain + shift

def dense(left, right):
    return jnp.dot(left, right, precision=lax.Precision.HIGHEST, preferred_element_type=jnp.float32)

def dense_t(left, right):
    return lax.dot_general(left, right, (((1,), (1,)), ((), ())), precision=lax.Precision.HIGHEST, preferred_element_type=jnp.float32)

def attention(queries, keys_all, values_all, segment_row):
    q_block = min(512, LEN)
    scale = HEAD_DIM ** (-0.5)
    q_heads = queries.reshape(LEN // q_block, q_block, HEADS, HEAD_DIM)
    k_heads = keys_all.reshape(LEN, HEADS, HEAD_DIM)
    v_heads = values_all.reshape(LEN, HEADS, HEAD_DIM)
    positions = jnp.arange(LEN, dtype=jnp.int32)

    def one_block(members):
        q_part, q_start = members
        scores = jnp.einsum('qhd,khd->hqk', q_part, k_heads, precision=lax.Precision.HIGHEST) * scale
        scores = low_back(scores)
        q_pos = q_start + jnp.arange(q_block, dtype=jnp.int32)
        q_seg = lax.dynamic_slice_in_dim(segment_row, q_start, q_block)
        allowed = (positions[None, :] <= q_pos[:, None]) & (segment_row[None, :] == q_seg[:, None])
        masked = jnp.where(allowed[None], scores, -1e+30)
        highest = lax.optimization_barrier(jnp.max(masked, axis=-1, keepdims=True))
        raised = jnp.where(allowed[None], jnp.exp(masked - highest), 0.0)
        probabilities = low(raised / lax.optimization_barrier(jnp.sum(raised, axis=-1, keepdims=True)))
        return jnp.einsum('hqk,khd->qhd', probabilities, v_heads, precision=lax.Precision.HIGHEST)
    starts = jnp.arange(LEN // q_block, dtype=jnp.int32) * q_block
    blocks = lax.map(jax.checkpoint(one_block), (q_heads, starts))
    return blocks.reshape(LEN, D)

def one_row(row_in, segment_row, active_row, weights):
    gain_one, bias_one, w_qkv, b_qv, w_out, b_out, gain_two, bias_two, w_up, b_up, w_down, b_down = weights
    normed = low(layer_norm(row_in, gain_one, bias_one))
    joined = dense(normed, w_qkv)
    queries = low(low_back(joined[:, :D] + b_qv[:D]))
    keys_all = low(low_back(joined[:, D:2 * D]))
    values_all = low(low_back(joined[:, 2 * D:] + b_qv[D:]))
    mixed = low(low_back(attention(queries, keys_all, values_all, segment_row)))
    branch = low_back(dense(mixed, w_out) + b_out)
    middle = row_in + active_row[:, None] * branch
    normed_two = low(layer_norm(middle, gain_two, bias_two))
    before = low_back(dense_t(normed_two, w_up) + b_up)
    hidden = low(jax.nn.gelu(before, approximate=True))
    feed = low_back(dense(hidden, w_down) + b_down)
    return middle + active_row[:, None] * feed

def reference(tokens, cotangent, segment_ids, exit_mask, ln1_gain, ln1_bias, w_qkv, b_qv, w_out, b_out, ln2_gain, ln2_bias, w_up, b_up, w_down, b_down):
    active = jnp.repeat(exit_mask, TILE, axis=1).astype(jnp.float32)
    params = tuple((member.astype(jnp.float32) for member in (ln1_gain, ln1_bias, w_qkv, b_qv, w_out, b_out, ln2_gain, ln2_bias, w_up, b_up, w_down, b_down)))

    def forward(inputs, weights):

        def row_step(members):
            row_in, segment_row, active_row = members
            return one_row(row_in, segment_row, active_row, weights)
        return lax.map(jax.checkpoint(row_step), (inputs, segment_ids, active))
    output, pullback = jax.vjp(forward, tokens.astype(jnp.float32), params)
    input_grad, grads = pullback(cotangent.astype(jnp.float32))
    return (output.astype(jnp.bfloat16), input_grad, grads[0], grads[1], grads[2], grads[3], grads[4], grads[5], grads[6], grads[7], grads[8], grads[9], grads[10], grads[11])
```

```python
import functools

import jax
import jax.numpy as jnp
from jax import lax
from jax.experimental import pallas as pl
from jax.experimental.pallas import tpu as pltpu
from jax.sharding import PartitionSpec as P

HEADS = 32
HEAD_DIM = 64
TILE = 128
PAIR = 2 * HEAD_DIM
Q_BLOCK = 256
PAD = 16
EPSILON = 1e-05
GELU_C = 0.7978845608028654
GELU_K = 0.044715
NEGATIVE = -1e30
VMEM_LIMIT = 56 * 1024 * 1024
LOW = jnp.bfloat16
WIDE = jnp.float32


def product(left, right):
    return jnp.dot(left, right, preferred_element_type=WIDE)


def product_t(left, right):
    return lax.dot_general(left, right, (((1,), (1,)), ((), ())), preferred_element_type=WIDE)


def product_rows(left, right):
    return lax.dot_general(left, right, (((0,), (0,)), ((), ())), preferred_element_type=WIDE)


def norm_stats(values):
    centre = jnp.mean(values, axis=-1, keepdims=True)
    centred = values - centre
    spread = jnp.mean(centred * centred, axis=-1, keepdims=True)
    return centre, lax.rsqrt(spread + EPSILON)


def norm_backward(upstream, normed, inverse, gain):
    graded = upstream * gain
    first = jnp.mean(graded, axis=-1, keepdims=True)
    second = jnp.mean(graded * normed, axis=-1, keepdims=True)
    return inverse * (graded - first - normed * second)


def flip(values, axis, bit, size):
    return lax.ppermute(values, axis, [(i, i ^ bit) for i in range(size)])


def gather_seq(values, n_seq):
    if n_seq != 4:
        return lax.all_gather(values, "seq", axis=0, tiled=False)
    me = lax.axis_index("seq")
    half = values.shape[0] // 2
    one = flip(values, "seq", 1, 4)
    two = flip(values, "seq", 2, 4)
    low = flip(one[:half], "seq", 2, 4)
    high = flip(two[half:], "seq", 1, 4)
    out = jnp.zeros((4,) + values.shape, values.dtype)
    zero = jnp.zeros((), me.dtype)
    out = lax.dynamic_update_slice(out, values[None], (me, zero, zero))
    out = lax.dynamic_update_slice(out, one[None], (me ^ 1, zero, zero))
    out = lax.dynamic_update_slice(out, two[None], (me ^ 2, zero, zero))
    out = lax.dynamic_update_slice(out, low[None], (me ^ 3, zero, zero))
    return lax.dynamic_update_slice(out, high[None], (me ^ 3, zero + half, zero))


def scatter_seq(values, n_seq):
    n = values.shape[0] // n_seq
    me = lax.axis_index("seq")
    if n_seq != 4:
        parts = lax.all_to_all(values.astype(LOW).reshape(n_seq, n, -1), "seq", 0, 0, tiled=True)
        return jnp.sum(parts.astype(WIDE), axis=0)
    total = lax.dynamic_slice_in_dim(values, me * n, n, 0)
    parts = []
    for bit in (3, 1, 2):
        piece = lax.dynamic_slice_in_dim(values, (me ^ bit) * n, n, 0).astype(LOW)
        parts.append(flip(piece, "seq", bit, 4))
    for part in parts:
        total = total + part.astype(WIDE)
    return total


def key_range(q_start, q_count, length):
    low = max(0, (q_start - (length // 2 - 1)) // q_count * q_count)
    return low, q_start + q_count


def block_mask(starts, low, high, q_start, q_count):
    shape = (high - low, q_count)
    key = low + lax.broadcasted_iota(jnp.int32, shape, 0)
    query = q_start + lax.broadcasted_iota(jnp.int32, shape, 1)
    return (key <= query) & (key >= starts)


def attend_kernel(q_ref, k_ref, v_ref, start_ref, o_ref, lse_ref):
    length = q_ref.shape[0]
    lane = lax.broadcasted_iota(jnp.int32, (1, PAIR), 1)
    row = lax.broadcasted_iota(jnp.int32, (PAIR, 1), 0)
    for q_start in range(0, length, Q_BLOCK):
        low, high = key_range(q_start, Q_BLOCK, length)
        here = slice(q_start, q_start + Q_BLOCK)
        q, k, v = q_ref[here, :], k_ref[low:high, :], v_ref[low:high, :]
        allowed = block_mask(start_ref[:, here], low, high, q_start, Q_BLOCK)
        mixed = []
        for head in range(2):
            mine = (lane >= head * HEAD_DIM) & (lane < (head + 1) * HEAD_DIM)
            q_head = jnp.where(mine, q, jnp.zeros_like(q))
            scores = product_t(k, q_head) * HEAD_DIM ** (-0.5)
            scores = jnp.where(allowed, scores, NEGATIVE)
            peak = jnp.max(scores, axis=0, keepdims=True)
            raised = jnp.exp(scores - peak)
            total = jnp.sum(raised, axis=0, keepdims=True)
            probs = (raised / total).astype(LOW)
            mixed.append(product_rows(v, probs))
            lse_ref[0, head : head + 1, here] = peak + jnp.log(total)
        joined = jnp.where(row < HEAD_DIM, mixed[0], mixed[1])
        o_ref[here, :] = joined.T.astype(LOW)


def attend(qkv, starts, width):
    length = qkv.shape[0]
    pairs = width // PAIR
    return pl.pallas_call(
        attend_kernel,
        grid=(pairs,),
        in_specs=[
            pl.BlockSpec((length, PAIR), lambda j: (0, j)),
            pl.BlockSpec((length, PAIR), lambda j: (0, pairs + j)),
            pl.BlockSpec((length, PAIR), lambda j: (0, 2 * pairs + j)),
            pl.BlockSpec((1, length), lambda j: (0, 0)),
        ],
        out_specs=[
            pl.BlockSpec((length, PAIR), lambda j: (0, j)),
            pl.BlockSpec((1, 2, length), lambda j: (j, 0, 0)),
        ],
        out_shape=[
            jax.ShapeDtypeStruct((length, width), LOW),
            jax.ShapeDtypeStruct((pairs, 2, length), WIDE),
        ],
        compiler_params=pltpu.CompilerParams(vmem_limit_bytes=VMEM_LIMIT),
        cost_estimate=pl.CostEstimate(
            flops=16 * length * length * width,
            bytes_accessed=8 * length * width,
            transcendentals=length * length * width // HEAD_DIM,
        ),
        name="attend",
    )(qkv, qkv, qkv, starts)


def attend_back_kernel(q_ref, k_ref, v_ref, do_ref, start_ref, lse_ref, out_ref, dk_acc, dv_acc):
    length = q_ref.shape[0]
    width = out_ref.shape[1] // 3
    at = pl.program_id(0) * PAIR
    scale = HEAD_DIM ** (-0.5)
    lane = lax.broadcasted_iota(jnp.int32, (1, PAIR), 1)
    row = lax.broadcasted_iota(jnp.int32, (PAIR, 1), 0)
    dk_acc[...] = jnp.zeros_like(dk_acc)
    dv_acc[...] = jnp.zeros_like(dv_acc)
    for q_start in range(0, length, Q_BLOCK):
        low, high = key_range(q_start, Q_BLOCK, length)
        here = slice(q_start, q_start + Q_BLOCK)
        q, k, v, do = q_ref[here, :], k_ref[low:high, :], v_ref[low:high, :], do_ref[here, :]
        allowed = block_mask(start_ref[:, here], low, high, q_start, Q_BLOCK)
        d_query = []
        for head in range(2):
            mine = (lane >= head * HEAD_DIM) & (lane < (head + 1) * HEAD_DIM)
            q_head = jnp.where(mine, q, jnp.zeros_like(q))
            do_head = jnp.where(mine, do, jnp.zeros_like(do))
            scores = product_t(k, q_head) * scale - lse_ref[0, head : head + 1, here]
            probs = jnp.exp(jnp.where(allowed, scores, NEGATIVE))
            d_probs = product_t(v, do_head)
            delta = jnp.sum(probs * d_probs, axis=0, keepdims=True)
            d_scores = (probs * (d_probs - delta)).astype(LOW)
            d_query.append(product_rows(k, d_scores))
            dk_acc[low:high, :] += product(d_scores, q_head)
            dv_acc[low:high, :] += product(probs.astype(LOW), do_head)
        joined = jnp.where(row < HEAD_DIM, d_query[0], d_query[1]) * scale
        out_ref[here, pl.ds(pl.multiple_of(at, PAIR), PAIR)] = joined.T.astype(LOW)
    out_ref[:, pl.ds(pl.multiple_of(width + at, PAIR), PAIR)] = (dk_acc[...] * scale).astype(LOW)
    out_ref[:, pl.ds(pl.multiple_of(2 * width + at, PAIR), PAIR)] = dv_acc[...].astype(LOW)


def attend_back(qkv, d_mixed, starts, logsum, width):
    length = qkv.shape[0]
    pairs = width // PAIR
    return pl.pallas_call(
        attend_back_kernel,
        grid=(pairs,),
        in_specs=[
            pl.BlockSpec((length, PAIR), lambda j: (0, j)),
            pl.BlockSpec((length, PAIR), lambda j: (0, pairs + j)),
            pl.BlockSpec((length, PAIR), lambda j: (0, 2 * pairs + j)),
            pl.BlockSpec((length, PAIR), lambda j: (0, j)),
            pl.BlockSpec((1, length), lambda j: (0, 0)),
            pl.BlockSpec((1, 2, length), lambda j: (j, 0, 0)),
        ],
        out_specs=pl.BlockSpec((length, 3 * width), lambda j: (0, 0)),
        out_shape=jax.ShapeDtypeStruct((length, 3 * width), LOW),
        scratch_shapes=[pltpu.VMEM((length, PAIR), WIDE), pltpu.VMEM((length, PAIR), WIDE)],
        compiler_params=pltpu.CompilerParams(vmem_limit_bytes=VMEM_LIMIT),
        cost_estimate=pl.CostEstimate(
            flops=40 * length * length * width,
            bytes_accessed=14 * length * width,
            transcendentals=length * length * width // HEAD_DIM,
        ),
        name="attend_back",
    )(qkv, qkv, qkv, d_mixed, starts, logsum)


def shards(
    n_seq,
    n_batch,
    tokens,
    cotangent,
    segment_ids,
    exit_mask,
    ln1_gain,
    ln1_bias,
    w_qkv,
    b_qv,
    w_out,
    b_out,
    ln2_gain,
    ln2_bias,
    w_up,
    b_up,
    w_down,
    b_down,
):
    _, local_len, width = tokens.shape
    length = n_seq * local_len
    own = w_qkv.shape[0]
    head_width = width // n_seq
    n_all = n_seq * n_batch
    me = lax.axis_index("seq")
    tokens = tokens.reshape(local_len, width)
    cotangent = cotangent.reshape(local_len, width)

    small_parts = (ln1_gain, ln1_bias, b_qv, b_out, ln2_gain, ln2_bias, b_up, b_down)
    sizes = [part.shape[0] for part in small_parts]
    n_small = sum(sizes)
    tiles = exit_mask.shape[1]
    small = jnp.concatenate(small_parts + (exit_mask.reshape(-1).astype(LOW),))
    small = jnp.pad(small, (0, 3 * head_width - small.shape[0]))

    by_head = w_qkv.reshape(own, 3, n_seq, head_width).transpose(2, 0, 1, 3)
    by_head = by_head.reshape(n_seq, own, 3 * head_width)
    extra = jnp.broadcast_to(small[None, None], (n_seq, PAD, 3 * head_width))
    moved = lax.all_to_all(jnp.concatenate([by_head, extra], axis=1), "seq", 0, 0, tiled=True)
    small_rows = moved[:, own, :]
    active_row = jnp.repeat(small_rows[:, n_small : n_small + tiles].reshape(-1), TILE)
    active_row = active_row.astype(WIDE).reshape(length, 1)
    sent = jnp.concatenate(
        [
            moved[:, :own].reshape(n_seq * own, 3 * head_width),
            small_rows,
            jnp.zeros((PAD - n_seq % PAD if n_seq % PAD else 0, 3 * head_width), LOW),
        ],
        axis=0,
    )
    out_part = lax.all_gather(w_out, "batch", axis=0, tiled=True)
    joined = lax.all_gather(sent, "batch", axis=0, tiled=False)
    qkv_full = joined[:, : n_seq * own].reshape(n_batch, n_seq, own, 3 * head_width)
    qkv_full = qkv_full.transpose(1, 0, 2, 3).reshape(width, 3 * head_width)
    small_all = joined[:, n_seq * own : n_seq * own + n_seq, :n_small]
    small_all = small_all.transpose(1, 0, 2).astype(WIDE)
    params, at = [], 0
    for size in sizes:
        params.append(small_all[:, :, at : at + size].reshape(-1))
        at += size
    gain_one, bias_one, qv_bias, out_bias, gain_two, bias_two, up_bias_all, down_bias = params
    up_all = lax.all_gather(w_up, "batch", axis=0, tiled=True)
    down_all = lax.all_gather(w_down, "batch", axis=0, tiled=True)
    hidden_count = up_all.shape[0]
    up_bias = lax.dynamic_slice_in_dim(up_bias_all, me * hidden_count, hidden_count)

    out_full = gather_seq(out_part, n_seq).reshape(width, width)

    row_low = gather_seq(tokens, n_seq).reshape(length, width)
    row = row_low.astype(WIDE)
    centre_one, inverse_one = norm_stats(row)
    normed_one = (row - centre_one) * inverse_one
    normed_low = (normed_one * gain_one + bias_one).astype(LOW)
    own_q = lax.dynamic_slice_in_dim(qv_bias, me * head_width, head_width)
    own_v = lax.dynamic_slice_in_dim(qv_bias, width + me * head_width, head_width)
    own_bias = jnp.concatenate([own_q, jnp.zeros_like(own_q), own_v])
    qkv = (product(normed_low, qkv_full) + own_bias).astype(LOW)
    segment_row = segment_ids.reshape(length)
    starts = jnp.sum(
        (segment_row[None, :] < segment_row[:, None]).astype(jnp.int32), axis=1
    ).reshape(1, length)
    mixed, logsum = attend(qkv, starts, head_width)
    mixed_all = gather_seq(mixed, n_seq).transpose(1, 0, 2).reshape(length, width)
    branch = product(mixed_all, out_full) + out_bias
    middle = row + active_row * branch
    centre_two, inverse_two = norm_stats(middle)
    normed_two = (middle - centre_two) * inverse_two
    normed_two_low = (normed_two * gain_two + bias_two).astype(LOW)

    active = jnp.repeat(exit_mask.reshape(-1), TILE).astype(WIDE).reshape(local_len, 1)
    grad_low = (cotangent.astype(WIDE) * active).astype(LOW)
    grad_row = gather_seq(grad_low, n_seq).reshape(length, width)
    before = product_t(normed_two_low, up_all) + up_bias
    inner = GELU_C * (before + GELU_K * before * before * before)
    tangent = jnp.tanh(inner)
    hidden_low = (0.5 * before * (1.0 + tangent)).astype(LOW)
    slope = 0.5 * (1.0 + tangent) + 0.5 * before * (1.0 - tangent * tangent) * GELU_C * (
        1.0 + 3.0 * GELU_K * before * before
    )
    grad_down = lax.psum_scatter(
        product_rows(hidden_low, grad_row).astype(LOW), "batch", scatter_dimension=0, tiled=True
    )
    d_before = (product_t(grad_row, down_all) * slope).astype(LOW)
    d_normed_two = scatter_seq(product(d_before, up_all), n_seq)
    grad_up = lax.psum_scatter(
        product_rows(d_before, normed_two_low).astype(LOW), "batch", scatter_dimension=0, tiled=True
    )
    grad_upb = jnp.sum(d_before.astype(WIDE), axis=0)
    grad_downb = jnp.sum(
        lax.dynamic_slice_in_dim(grad_row, me * head_width, head_width, 1).astype(WIDE), axis=0
    )
    feed = scatter_seq(product(hidden_low, down_all), n_seq) + down_bias
    middle_own = lax.dynamic_slice_in_dim(middle, me * local_len, local_len, 0)
    layer_out = (middle_own + active * feed).astype(LOW)

    normed_own = lax.dynamic_slice_in_dim(normed_two, me * local_len, local_len, 0)
    inverse_own = lax.dynamic_slice_in_dim(inverse_two, me * local_len, local_len, 0)
    d_middle = cotangent.astype(WIDE) + norm_backward(d_normed_two, normed_own, inverse_own, gain_two)
    grad_gain_two = jnp.sum(d_normed_two * normed_own, axis=0)
    grad_bias_two = jnp.sum(d_normed_two, axis=0)
    d_branch = (d_middle * active).astype(LOW)
    d_mixed_own = product_t(d_branch, out_full).astype(LOW)
    d_mixed = lax.all_to_all(d_mixed_own, "seq", 1, 0, tiled=True)
    d_qkv = attend_back(qkv, d_mixed, starts, logsum, head_width)
    d_branch_row = gather_seq(d_branch, n_seq).reshape(length, width)
    grad_out = lax.psum_scatter(
        product_rows(mixed, d_branch_row).astype(LOW), "batch", scatter_dimension=0, tiled=True
    )
    grad_outb = jnp.sum(
        lax.dynamic_slice_in_dim(d_branch_row, me * head_width, head_width, 1).astype(WIDE), axis=0
    )

    d_normed_part = product_t(d_qkv, qkv_full)
    grad_gain_one = jnp.sum(d_normed_part * normed_one, axis=0)
    grad_bias_one = jnp.sum(d_normed_part, axis=0)
    d_normed_one = scatter_seq(d_normed_part, n_seq)
    row_own = tokens.astype(WIDE)
    centre_own, inverse_first = norm_stats(row_own)
    d_input = d_middle + norm_backward(
        d_normed_one, (row_own - centre_own) * inverse_first, inverse_first, gain_one
    )

    def place(values, total):
        return lax.dynamic_update_slice_in_dim(
            jnp.zeros((total,), WIDE), values, me * values.shape[0], 0
        )

    d_bias = jnp.sum(d_qkv.astype(WIDE), axis=0)
    grad_qvb = jnp.concatenate(
        [place(d_bias[:head_width], width), place(d_bias[2 * head_width :], width)]
    )
    small_grads = (
        grad_gain_one,
        grad_bias_one,
        grad_qvb,
        place(grad_outb, width),
        grad_gain_two,
        grad_bias_two,
        place(grad_upb, n_seq * hidden_count),
        place(grad_downb, width),
    )
    packed = jnp.concatenate([g.reshape(n_seq, n_batch, -1) for g in small_grads], axis=2)
    packed = jnp.pad(packed, ((0, 0), (0, 0), (0, 3 * head_width - n_small))).astype(LOW)
    grad_qkv_part = product_rows(normed_low, d_qkv).astype(LOW)
    grad_qkv_part = grad_qkv_part.reshape(n_seq, n_batch, own, 3 * head_width)
    packed = jnp.pad(packed[:, :, None], ((0, 0), (0, 0), (0, PAD - 1), (0, 0)))
    grad_qkv_part = jnp.concatenate([grad_qkv_part, packed], axis=2).transpose(1, 0, 2, 3)
    reduced = lax.psum_scatter(
        grad_qkv_part.reshape(n_batch * n_seq * (own + PAD), 3 * head_width),
        "batch",
        scatter_dimension=0,
        tiled=True,
    )
    final = lax.all_to_all(
        reduced.reshape(n_seq, own + PAD, 3 * head_width), "seq", 0, 0, tiled=True
    )
    grad_qkv = final[:, :own].reshape(n_seq, own, 3, head_width).transpose(1, 2, 0, 3)
    grad_qkv = grad_qkv.reshape(own, 3 * width).astype(WIDE)
    small_out = jnp.sum(final[:, own, :n_small].astype(WIDE), axis=0)
    small_result, at = [], 0
    for size in sizes:
        small_result.append(small_out[at : at + size])
        at += size
    g_one, c_one, g_qvb, g_outb, g_two, c_two, g_upb, g_downb = small_result
    return (
        layer_out[None],
        d_input[None],
        g_one,
        c_one,
        grad_qkv,
        g_qvb,
        grad_out.astype(WIDE),
        g_outb,
        g_two,
        c_two,
        grad_up.astype(WIDE),
        g_upb,
        grad_down.astype(WIDE),
        g_downb,
    )


def solution(mesh):
    vector = P(("seq", "batch"))
    matrix = P(("seq", "batch"), None)
    rows = P("batch", "seq", None)
    return jax.shard_map(
        functools.partial(shards, mesh.shape["seq"], mesh.shape["batch"]),
        mesh=mesh,
        in_specs=(
            rows, rows, P("batch", None), P("batch", "seq"),
            vector, vector, matrix, vector, matrix, vector, vector, vector, matrix, vector, matrix, vector,
        ),
        out_specs=(
            rows, rows, vector, vector, matrix, vector, matrix, vector, vector, vector, matrix, vector, matrix, vector,
        ),
        check_vma=False,
    )
```

```python
import functools

import jax
import jax.numpy as jnp
from jax import lax
from jax.experimental import pallas as pl
from jax.experimental.pallas import tpu as pltpu
from jax.sharding import PartitionSpec as P

HEADS = 32
HEAD_DIM = 64
TILE = 128
PAIR = 2 * HEAD_DIM
Q_BLOCK = 256
FFN_ROWS = 512
EXTRA = 128
EPSILON = 1e-05
GELU_C = 0.7978845608028654
GELU_K = 0.044715
NEGATIVE = -1e30
VMEM_LIMIT = 56 * 1024 * 1024
LOW = jnp.bfloat16
WIDE = jnp.float32


def product(left, right):
    return jnp.dot(left, right, preferred_element_type=WIDE)


def product_t(left, right):
    return lax.dot_general(left, right, (((1,), (1,)), ((), ())), preferred_element_type=WIDE)


def product_rows(left, right):
    return lax.dot_general(left, right, (((0,), (0,)), ((), ())), preferred_element_type=WIDE)


def norm_stats(values):
    centre = jnp.mean(values, axis=-1, keepdims=True)
    centred = values - centre
    spread = jnp.mean(centred * centred, axis=-1, keepdims=True)
    return centre, lax.rsqrt(spread + EPSILON)


def norm_backward(upstream, normed, inverse, gain):
    graded = upstream * gain
    first = jnp.mean(graded, axis=-1, keepdims=True)
    second = jnp.mean(graded * normed, axis=-1, keepdims=True)
    return inverse * (graded - first - normed * second)


def flip(values, axis, bit, size):
    return lax.ppermute(values, axis, [(i, i ^ bit) for i in range(size)])


def tie(*values):
    return lax.optimization_barrier(values)


def gather_start(values, n_seq):
    if n_seq != 4:
        return [values] + [flip(values, "seq", bit, n_seq) for bit in range(1, n_seq)]
    return [values, flip(values, "seq", 1, 4), flip(values, "seq", 2, 4)]


def gather_end(held, n_seq):
    if n_seq != 4:
        return held
    values, one, two = held
    half = values.shape[0] // 2
    low = flip(one[:half], "seq", 2, 4)
    high = flip(two[half:], "seq", 1, 4)
    return [values, one, two, jnp.concatenate([low, high], axis=0)]


def exchange(blocks, n_seq):
    return [blocks[0]] + [flip(blocks[bit], "seq", bit, n_seq) for bit in range(1, n_seq)]


def scatter_split(values, n_seq):
    count = values.shape[0] // n_seq
    if n_seq != 4:
        return [values[bit * count : (bit + 1) * count] for bit in range(n_seq)]
    half = count // 2

    def piece(bit, part):
        return values[bit * count + part * half : bit * count + (part + 1) * half]

    return [
        values[:count],
        jnp.concatenate([piece(1, 0), piece(3, 0)], axis=0),
        jnp.concatenate([piece(2, 1), piece(3, 1)], axis=0),
        piece(2, 0),
        piece(1, 1),
    ]


def scatter_send(blocks, n_seq):
    if n_seq != 4:
        return [[block] for block in exchange(blocks, n_seq)]
    own, first, second, then_second, then_first = blocks
    half = own.shape[0] // 2
    first, second = flip(first, "seq", 1, 4), flip(second, "seq", 2, 4)
    then_second = (then_second.astype(WIDE) + first[half:].astype(WIDE)).astype(LOW)
    then_first = (then_first.astype(WIDE) + second[half:].astype(WIDE)).astype(LOW)
    then_second, then_first = flip(then_second, "seq", 2, 4), flip(then_first, "seq", 1, 4)
    return [[own], [first, second], [then_second, then_first]]


def scatter_end(parts):
    count = parts[0][0].shape[0]
    total = parts[0][0].astype(WIDE)
    for part in parts[1:]:
        rows = count // len(part)
        total = total + jnp.concatenate([piece[:rows] for piece in part], axis=0).astype(WIDE)
    return total


def pair_split(left, n_batch):
    side = lax.axis_index("batch") & 1
    blocks = left.reshape(left.shape[0], n_batch // 2, 2, left.shape[1] // n_batch)
    sent = lax.dynamic_index_in_dim(blocks, 1 - side, 2, False)
    kept = lax.dynamic_index_in_dim(blocks, side, 2, False)
    return sent.reshape(left.shape[0], -1), kept.reshape(left.shape[0], -1)


def rows_kernel(side_ref, left_ref, right_ref, *refs):
    total = product_rows(left_ref[...], right_ref[...])
    if len(refs) == 2:
        total += refs[0][...].astype(WIDE)
    refs[-1][...] = total.astype(LOW)


def rows_product(side, left, right, added, n_batch):
    length, columns = left.shape
    width = right.shape[1]
    count = columns // n_batch
    block = pl.BlockSpec((count, width), lambda k, side: (k, 0))
    return pl.pallas_call(
        rows_kernel,
        grid_spec=pltpu.PrefetchScalarGridSpec(
            num_scalar_prefetch=1,
            grid=(n_batch // 2,),
            in_specs=[
                pl.BlockSpec((length, count), lambda k, side: (0, 2 * k + side[0])),
                pl.BlockSpec((length, width), lambda k, side: (0, 0), pipeline_mode=pl.Buffered(1)),
            ]
            + [block] * len(added),
            out_specs=block,
        ),
        out_shape=jax.ShapeDtypeStruct((columns // 2, width), LOW),
        compiler_params=pltpu.CompilerParams(vmem_limit_bytes=VMEM_LIMIT),
        cost_estimate=pl.CostEstimate(flops=length * width, bytes_accessed=length, transcendentals=0),
        name="rows_product",
    )(side, left, right, *added)


def pair_rows(left, right, n_batch):
    if left.shape[1] // n_batch % 128:
        return pair_product(*pair_split(left, n_batch), right, n_batch)
    side = (lax.axis_index("batch") & 1).reshape(1)
    moved = flip(rows_product(1 - side, left, right, (), n_batch), "batch", 1, n_batch)
    return rows_product(side, left, right, (moved,), n_batch)


def pair_product(sent, kept, right, n_batch):
    moved = flip(product_rows(sent, right).astype(LOW), "batch", 1, n_batch)
    return (product_rows(kept, right) + moved.astype(WIDE)).astype(LOW)


def scatter_batch(total, n_batch):
    groups = [list(range(0, n_batch, 2)), list(range(1, n_batch, 2))]
    return lax.psum_scatter(
        total,
        "batch",
        scatter_dimension=0,
        tiled=True,
        axis_index_groups=groups,
    )


def key_range(q_start, q_count, length):
    low = max(0, (q_start - (length // 2 - 1)) // q_count * q_count)
    return low, q_start + q_count


def block_mask(starts, low, high, q_start, q_count):
    shape = (high - low, q_count)
    key = low + lax.broadcasted_iota(jnp.int32, shape, 0)
    query = q_start + lax.broadcasted_iota(jnp.int32, shape, 1)
    return (key <= query) & (key >= starts)


def load_natural(me, pairs):
    for source, target in pairs:
        for block in range(target.shape[0] // Q_BLOCK):
            at = pl.multiple_of((block ^ me) * Q_BLOCK, Q_BLOCK)
            target[block * Q_BLOCK : (block + 1) * Q_BLOCK, :] = source[pl.ds(at, Q_BLOCK), :]


def attend_kernel(me_ref, q_ref, k_ref, v_ref, start_ref, o_ref, lse_ref, k_own, v_own):
    length = q_ref.shape[0]
    me = me_ref[0]
    load_natural(me, ((k_ref, k_own), (v_ref, v_own)))
    lane = lax.broadcasted_iota(jnp.int32, (1, PAIR), 1)
    row = lax.broadcasted_iota(jnp.int32, (PAIR, 1), 0)
    for q_start in range(0, length, Q_BLOCK):
        low, high = key_range(q_start, Q_BLOCK, length)
        here = slice(q_start, q_start + Q_BLOCK)
        there = pl.ds(pl.multiple_of((q_start // Q_BLOCK ^ me) * Q_BLOCK, Q_BLOCK), Q_BLOCK)
        q, k, v = q_ref[there, :], k_own[low:high, :], v_own[low:high, :]
        allowed = block_mask(start_ref[:, here], low, high, q_start, Q_BLOCK)
        mixed = []
        for head in range(2):
            mine = (lane >= head * HEAD_DIM) & (lane < (head + 1) * HEAD_DIM)
            q_head = jnp.where(mine, q, jnp.zeros_like(q))
            scores = product_t(k, q_head) * HEAD_DIM ** (-0.5)
            scores = jnp.where(allowed, scores, NEGATIVE)
            peak = jnp.max(scores, axis=0, keepdims=True)
            raised = jnp.exp(scores - peak)
            total = jnp.sum(raised, axis=0, keepdims=True)
            probs = (raised / total).astype(LOW)
            mixed.append(product_rows(v, probs))
            lse_ref[0, head : head + 1, here] = peak + jnp.log(total)
        joined = jnp.where(row < HEAD_DIM, mixed[0], mixed[1])
        o_ref[there, :] = joined.T.astype(LOW)


def attend(me, qkv, starts, width):
    length = qkv.shape[0]
    pairs = width // PAIR
    return pl.pallas_call(
        attend_kernel,
        grid_spec=pltpu.PrefetchScalarGridSpec(
            num_scalar_prefetch=1,
            grid=(pairs,),
            in_specs=[
                pl.BlockSpec((length, PAIR), lambda j, me: (0, j)),
                pl.BlockSpec((length, PAIR), lambda j, me: (0, pairs + j)),
                pl.BlockSpec((length, PAIR), lambda j, me: (0, 2 * pairs + j)),
                pl.BlockSpec((1, length), lambda j, me: (0, 0)),
            ],
            out_specs=[
                pl.BlockSpec((length, PAIR), lambda j, me: (0, j)),
                pl.BlockSpec((1, 2, length), lambda j, me: (j, 0, 0)),
            ],
            scratch_shapes=[pltpu.VMEM((length, PAIR), LOW), pltpu.VMEM((length, PAIR), LOW)],
        ),
        out_shape=[
            jax.ShapeDtypeStruct((length, width), LOW),
            jax.ShapeDtypeStruct((pairs, 2, length), WIDE),
        ],
        compiler_params=pltpu.CompilerParams(vmem_limit_bytes=VMEM_LIMIT),
        cost_estimate=pl.CostEstimate(
            flops=16 * length * length * width,
            bytes_accessed=8 * length * width,
            transcendentals=length * length * width // HEAD_DIM,
        ),
        name="attend",
    )(me, qkv, qkv, qkv, starts)


def attend_back_kernel(
    me_ref, q_ref, k_ref, v_ref, do_ref, start_ref, lse_ref, out_ref, k_own, v_own, dk_acc, dv_acc
):
    length = q_ref.shape[0]
    width = out_ref.shape[1] // 3
    me = me_ref[0]
    at = pl.program_id(0) * PAIR
    scale = HEAD_DIM ** (-0.5)
    lane = lax.broadcasted_iota(jnp.int32, (1, PAIR), 1)
    row = lax.broadcasted_iota(jnp.int32, (PAIR, 1), 0)
    load_natural(me, ((k_ref, k_own), (v_ref, v_own)))
    dk_acc[...] = jnp.zeros_like(dk_acc)
    dv_acc[...] = jnp.zeros_like(dv_acc)
    for q_start in range(0, length, Q_BLOCK):
        low, high = key_range(q_start, Q_BLOCK, length)
        here = slice(q_start, q_start + Q_BLOCK)
        there = pl.ds(pl.multiple_of((q_start // Q_BLOCK ^ me) * Q_BLOCK, Q_BLOCK), Q_BLOCK)
        q, k, v, do = q_ref[there, :], k_own[low:high, :], v_own[low:high, :], do_ref[there, :]
        allowed = block_mask(start_ref[:, here], low, high, q_start, Q_BLOCK)
        d_query = []
        for head in range(2):
            mine = (lane >= head * HEAD_DIM) & (lane < (head + 1) * HEAD_DIM)
            q_head = jnp.where(mine, q, jnp.zeros_like(q))
            do_head = jnp.where(mine, do, jnp.zeros_like(do))
            scores = product_t(k, q_head) * scale - lse_ref[0, head : head + 1, here]
            probs = jnp.exp(jnp.where(allowed, scores, NEGATIVE))
            d_probs = product_t(v, do_head)
            delta = jnp.sum(probs * d_probs, axis=0, keepdims=True)
            d_scores = (probs * (d_probs - delta)).astype(LOW)
            d_query.append(product_rows(k, d_scores))
            dk_acc[low:high, :] += product(d_scores, q_head)
            dv_acc[low:high, :] += product(probs.astype(LOW), do_head)
        joined = jnp.where(row < HEAD_DIM, d_query[0], d_query[1]) * scale
        out_ref[there, pl.ds(pl.multiple_of(at, PAIR), PAIR)] = joined.T.astype(LOW)
    for q_start in range(0, length, Q_BLOCK):
        here = slice(q_start, q_start + Q_BLOCK)
        there = pl.ds(pl.multiple_of((q_start // Q_BLOCK ^ me) * Q_BLOCK, Q_BLOCK), Q_BLOCK)
        d_key = (dk_acc[here, :] * scale).astype(LOW)
        out_ref[there, pl.ds(pl.multiple_of(width + at, PAIR), PAIR)] = d_key
        d_value = dv_acc[here, :].astype(LOW)
        out_ref[there, pl.ds(pl.multiple_of(2 * width + at, PAIR), PAIR)] = d_value


def attend_back(me, qkv, d_mixed, starts, logsum, width):
    length = qkv.shape[0]
    pairs = width // PAIR
    return pl.pallas_call(
        attend_back_kernel,
        grid_spec=pltpu.PrefetchScalarGridSpec(
            num_scalar_prefetch=1,
            grid=(pairs,),
            in_specs=[
                pl.BlockSpec((length, PAIR), lambda j, me: (0, j)),
                pl.BlockSpec((length, PAIR), lambda j, me: (0, pairs + j)),
                pl.BlockSpec((length, PAIR), lambda j, me: (0, 2 * pairs + j)),
                pl.BlockSpec((length, PAIR), lambda j, me: (0, j)),
                pl.BlockSpec((1, length), lambda j, me: (0, 0)),
                pl.BlockSpec((1, 2, length), lambda j, me: (j, 0, 0)),
            ],
            out_specs=pl.BlockSpec((length, 3 * width), lambda j, me: (0, 0)),
            scratch_shapes=[
                pltpu.VMEM((length, PAIR), LOW),
                pltpu.VMEM((length, PAIR), LOW),
                pltpu.VMEM((length, PAIR), WIDE),
                pltpu.VMEM((length, PAIR), WIDE),
            ],
        ),
        out_shape=jax.ShapeDtypeStruct((length, 3 * width), LOW),
        compiler_params=pltpu.CompilerParams(vmem_limit_bytes=VMEM_LIMIT),
        cost_estimate=pl.CostEstimate(
            flops=40 * length * length * width,
            bytes_accessed=14 * length * width,
            transcendentals=length * length * width // HEAD_DIM,
        ),
        name="attend_back",
    )(me, qkv, qkv, qkv, d_mixed, starts, logsum)


def out_norm_kernel(n_seq, *refs):
    o_refs = refs[:n_seq]
    w_ref, row_ref, active_ref, bias_ref, gain_ref, shift_ref = refs[n_seq : n_seq + 6]
    low_ref, middle_ref, normed_ref, inverse_ref = refs[n_seq + 6 :]
    depth = o_refs[0].shape[1]
    branch = product(o_refs[0][...], w_ref[:depth, :])
    for block in range(1, n_seq):
        branch += product(o_refs[block][...], w_ref[block * depth : (block + 1) * depth, :])
    middle = row_ref[...].astype(WIDE) + active_ref[...] * (branch + bias_ref[...])
    centre, inverse = norm_stats(middle)
    normed = (middle - centre) * inverse
    low_ref[...] = (normed * gain_ref[...] + shift_ref[...]).astype(LOW)

    @pl.when(pl.program_id(0) == 0)
    def _():
        middle_ref[...] = middle
        normed_ref[...] = normed
        inverse_ref[...] = inverse


def out_norm(mixed_all, out_full, row_low, active_row, bias, gain, shift, n_seq):
    length, width = row_low.shape
    count = length // n_seq
    depth = width // n_seq

    def mixed_spec(bit):
        return pl.BlockSpec((count, depth), lambda k: (k ^ bit, 0))

    vector = pl.BlockSpec((1, width), lambda k: (0, 0))
    block = pl.BlockSpec((count, width), lambda k: (k, 0))
    first = pl.BlockSpec((count, width), lambda k: (0, 0))
    return pl.pallas_call(
        functools.partial(out_norm_kernel, n_seq),
        grid=(n_seq,),
        in_specs=[mixed_spec(bit) for bit in range(n_seq)]
        + [
            pl.BlockSpec((width, width), lambda k: (0, 0)),
            block,
            pl.BlockSpec((count, 1), lambda k: (k, 0)),
            vector,
            vector,
            vector,
        ],
        out_specs=[block, first, first, pl.BlockSpec((count, 1), lambda k: (0, 0))],
        out_shape=[
            jax.ShapeDtypeStruct((length, width), LOW),
            jax.ShapeDtypeStruct((count, width), WIDE),
            jax.ShapeDtypeStruct((count, width), WIDE),
            jax.ShapeDtypeStruct((count, 1), WIDE),
        ],
        compiler_params=pltpu.CompilerParams(vmem_limit_bytes=VMEM_LIMIT),
        cost_estimate=pl.CostEstimate(
            flops=2 * length * width * width,
            bytes_accessed=2 * width * width + 6 * length * width,
            transcendentals=length,
        ),
        name="out_norm",
    )(
        *mixed_all,
        out_full,
        row_low,
        active_row,
        bias.reshape(1, width),
        gain.reshape(1, width),
        shift.reshape(1, width),
    )


def assemble_kernel(me_ref, joined_ref, full_ref, extra_ref):
    own = joined_ref.shape[2]
    width = full_ref.shape[1]
    for member in range(joined_ref.shape[0]):
        rows = slice(member * own, (member + 1) * own)
        full_ref[rows, :] = joined_ref[member, 0, :, :width]
        extra_ref[rows, :] = joined_ref[member, 0, :, width:]


def assemble(me, joined, width):
    n_batch, n_seq, own, columns = joined.shape
    count = n_batch * own
    return pl.pallas_call(
        assemble_kernel,
        grid_spec=pltpu.PrefetchScalarGridSpec(
            num_scalar_prefetch=1,
            grid=(n_seq,),
            in_specs=[
                pl.BlockSpec((n_batch, 1, own, columns), lambda j, me: (0, j ^ me[0], 0, 0)),
            ],
            out_specs=[
                pl.BlockSpec((count, width), lambda j, me: (j, 0)),
                pl.BlockSpec((count, EXTRA), lambda j, me: (j, 0)),
            ],
        ),
        out_shape=[
            jax.ShapeDtypeStruct((n_seq * count, width), LOW),
            jax.ShapeDtypeStruct((n_seq * count, EXTRA), LOW),
        ],
        compiler_params=pltpu.CompilerParams(vmem_limit_bytes=VMEM_LIMIT),
        name="assemble",
    )(me, joined)


def ffn_up_kernel(n_ref, w_ref, bias_ref, hidden_ref, slope_ref):
    step = 512
    for at in range(0, w_ref.shape[0], step):
        here = slice(at, at + step)
        before = product_t(n_ref[...], w_ref[here, :]) + bias_ref[:, here]
        square = before * before
        tangent = jnp.tanh(before * (GELU_C + GELU_C * GELU_K * square))
        half = 0.5 + 0.5 * tangent
        hidden = before * half
        hidden_ref[:, here] = hidden.astype(LOW)
        slope_ref[:, here] = half + hidden * (1.0 - tangent) * (
            GELU_C + 3.0 * GELU_C * GELU_K * square
        )


def ffn_up(normed, w_up, bias):
    length, width = normed.shape
    hidden = w_up.shape[0]
    return pl.pallas_call(
        ffn_up_kernel,
        grid=(length // FFN_ROWS,),
        in_specs=[
            pl.BlockSpec((FFN_ROWS, width), lambda k: (k, 0)),
            pl.BlockSpec((hidden, width), lambda k: (0, 0), pipeline_mode=pl.Buffered(1)),
            pl.BlockSpec((1, hidden), lambda k: (0, 0)),
        ],
        out_specs=[
            pl.BlockSpec((FFN_ROWS, hidden), lambda k: (k, 0)),
            pl.BlockSpec((FFN_ROWS, hidden), lambda k: (k, 0)),
        ],
        out_shape=[
            jax.ShapeDtypeStruct((length, hidden), LOW),
            jax.ShapeDtypeStruct((length, hidden), WIDE),
        ],
        compiler_params=pltpu.CompilerParams(vmem_limit_bytes=VMEM_LIMIT),
        cost_estimate=pl.CostEstimate(
            flops=2 * length * width * hidden,
            bytes_accessed=2 * width * (hidden + length) + 6 * length * hidden,
            transcendentals=length * hidden,
        ),
        name="ffn_up",
    )(normed, w_up, bias.reshape(1, hidden))


def ffn_back_kernel(n_seq, grad_ref, slope_ref, down_ref, up_ref, d_before_ref, sum_ref, *refs):
    outs, (down, up, sems) = refs[:-3], refs[-3:]
    index = pl.program_id(0)
    load_down = pltpu.make_async_copy(down_ref, down, sems.at[0])
    load_up = pltpu.make_async_copy(up_ref, up, sems.at[1])

    @pl.when(index == 0)
    def _():
        load_down.start()
        load_up.start()
        sum_ref[...] = jnp.zeros_like(sum_ref)
        load_down.wait()

    step = 512
    for at in range(0, down.shape[0], step):
        here = slice(at, at + step)
        d_hidden = product_t(grad_ref[...], down[here, :])
        d_before = (d_hidden * slope_ref[:, here]).astype(LOW)
        d_before_ref[:, here] = d_before
        sum_ref[:, here] += jnp.sum(d_before.astype(WIDE), axis=0, keepdims=True)

    @pl.when(index == 0)
    def _():
        load_up.wait()

    d_normed = product(d_before_ref[...], up[...]).astype(LOW)
    half = d_normed.shape[0] // 2
    if n_seq != 4:
        places = [[(outs[bit], 0, slice(None))] for bit in range(n_seq)]
    else:
        own, first, second, then_second, then_first = outs
        upper, lower = slice(0, half), slice(half, 2 * half)
        places = [
            [(own, 0, slice(None))],
            [(first, 0, upper), (then_first, 0, lower)],
            [(then_second, 0, upper), (second, 0, lower)],
            [(first, half, upper), (second, half, lower)],
        ]
    for bit, targets in enumerate(places):

        @pl.when(index == bit)
        def _():
            for target, at, rows in targets:
                piece = d_normed[rows]
                target[at : at + piece.shape[0], :] = piece


def ffn_back(grad_row, slope, w_down, w_up, n_seq):
    length, width = grad_row.shape
    hidden = w_up.shape[0]
    count = length // n_seq
    sizes = [count] * n_seq if n_seq != 4 else [count, count, count, count // 2, count // 2]
    return pl.pallas_call(
        functools.partial(ffn_back_kernel, n_seq),
        grid=(n_seq,),
        in_specs=[
            pl.BlockSpec((count, width), lambda k: (k, 0)),
            pl.BlockSpec((count, hidden), lambda k: (k, 0)),
            pl.BlockSpec(memory_space=pl.ANY),
            pl.BlockSpec(memory_space=pl.ANY),
        ],
        out_specs=[
            pl.BlockSpec((count, hidden), lambda k: (k, 0)),
            pl.BlockSpec((1, hidden), lambda k: (0, 0)),
        ]
        + [pl.BlockSpec((size, width), lambda k: (0, 0)) for size in sizes],
        out_shape=[
            jax.ShapeDtypeStruct((length, hidden), LOW),
            jax.ShapeDtypeStruct((1, hidden), WIDE),
        ]
        + [jax.ShapeDtypeStruct((size, width), LOW) for size in sizes],
        scratch_shapes=[
            pltpu.VMEM((hidden, width), LOW),
            pltpu.VMEM((hidden, width), LOW),
            pltpu.SemaphoreType.DMA((2,)),
        ],
        compiler_params=pltpu.CompilerParams(vmem_limit_bytes=VMEM_LIMIT),
        cost_estimate=pl.CostEstimate(flops=length * width, bytes_accessed=length, transcendentals=0),
        name="ffn_back",
    )(grad_row, slope, w_down, w_up)


def norm_back_kernel(pieces, *refs):
    n_parts = sum(pieces)
    parts, at = [], 0
    for number in pieces:
        parts.append(refs[at : at + number])
        at += number
    cot_ref, normed_ref, inverse_ref, active_ref, gain_ref, w_ref = refs[n_parts : n_parts + 6]
    d_middle_ref, d_branch_ref, d_mixed_ref, sums_ref = refs[n_parts + 6 :]

    @pl.when(pl.program_id(0) == 0)
    def _():
        upstream = parts[0][0][...].astype(WIDE)
        for part in parts[1:]:
            upstream += jnp.concatenate([piece[...] for piece in part], axis=0).astype(WIDE)
        normed = normed_ref[...]
        d_middle = cot_ref[...].astype(WIDE) + norm_backward(
            upstream, normed, inverse_ref[...], gain_ref[...]
        )
        d_middle_ref[...] = d_middle
        d_branch = (d_middle * active_ref[...]).astype(LOW)
        d_branch_ref[...] = d_branch
        sums_ref[...] = jnp.zeros_like(sums_ref)
        sums_ref[0:1, :] = jnp.sum(upstream * normed, axis=0, keepdims=True)
        sums_ref[1:2, :] = jnp.sum(upstream, axis=0, keepdims=True)
        sums_ref[2:3, :] = jnp.sum(d_branch.astype(WIDE), axis=0, keepdims=True)

    d_mixed_ref[0] = product_t(d_branch_ref[...], w_ref[...]).astype(LOW)


def norm_back(parts, cotangent, normed, inverse, active, gain, out_full, n_seq):
    count, width = cotangent.shape
    depth = width // n_seq
    block = pl.BlockSpec((count, width), lambda j: (0, 0))
    column = pl.BlockSpec((count, 1), lambda j: (0, 0))
    return pl.pallas_call(
        functools.partial(norm_back_kernel, [len(part) for part in parts]),
        grid=(n_seq,),
        in_specs=[
            pl.BlockSpec((count // len(part), width), lambda j: (0, 0)) for part in parts for piece in part
        ]
        + [block, block]
        + [
            column,
            column,
            pl.BlockSpec((1, width), lambda j: (0, 0)),
            pl.BlockSpec((depth, width), lambda j: (j, 0)),
        ],
        out_specs=[
            block,
            block,
            pl.BlockSpec((1, count, depth), lambda j: (j, 0, 0)),
            pl.BlockSpec((8, width), lambda j: (0, 0)),
        ],
        out_shape=[
            jax.ShapeDtypeStruct((count, width), WIDE),
            jax.ShapeDtypeStruct((count, width), LOW),
            jax.ShapeDtypeStruct((n_seq, count, depth), LOW),
            jax.ShapeDtypeStruct((8, width), WIDE),
        ],
        compiler_params=pltpu.CompilerParams(vmem_limit_bytes=VMEM_LIMIT),
        cost_estimate=pl.CostEstimate(flops=count * width, bytes_accessed=count, transcendentals=0),
        name="norm_back",
    )(
        *[piece for part in parts for piece in part],
        cotangent,
        normed,
        inverse,
        active,
        gain.reshape(1, width),
        out_full,
    )


def format_kernel(n_seq, me_ref, *refs):
    out_ref = refs[n_seq]
    width = out_ref.shape[1] // 3
    count = width // n_seq
    for block in range(n_seq):
        ref = refs[block]
        for kind in range(3):
            at = kind * width + (me_ref[0] ^ block) * count
            at = pl.multiple_of(at, count)
            out_ref[:, pl.ds(at, count)] = ref[:, kind * count : (kind + 1) * count].astype(WIDE)


def format_qkv(me, blocks, width, n_seq):
    own = blocks[0].shape[0]
    return pl.pallas_call(
        functools.partial(format_kernel, n_seq),
        grid_spec=pltpu.PrefetchScalarGridSpec(
            num_scalar_prefetch=1,
            grid=(1,),
            in_specs=[pl.BlockSpec(blocks[0].shape, lambda i, me: (0, 0))] * n_seq,
            out_specs=pl.BlockSpec((own, 3 * width), lambda i, me: (0, 0)),
        ),
        out_shape=jax.ShapeDtypeStruct((own, 3 * width), WIDE),
        compiler_params=pltpu.CompilerParams(vmem_limit_bytes=VMEM_LIMIT),
        name="format_qkv",
    )(me, *blocks)


def gather_shared(values, n_seq, n_batch):
    half = values.shape[0] // 2
    side = lax.axis_index("batch") & 1
    mine = lax.dynamic_slice_in_dim(values, side * half, half, 0)
    held = gather_end(gather_start(mine, n_seq), n_seq)[1:]
    other = [flip(block, "batch", 1, n_batch) for block in held]
    blocks = [values]
    for mine, theirs in zip(held, other):
        blocks.append(jnp.where(side == 0, mine, theirs))
        blocks.append(jnp.where(side == 0, theirs, mine))
    return blocks


def shards(
    n_seq,
    n_batch,
    tokens,
    cotangent,
    segment_ids,
    exit_mask,
    ln1_gain,
    ln1_bias,
    w_qkv,
    b_qv,
    w_out,
    b_out,
    ln2_gain,
    ln2_bias,
    w_up,
    b_up,
    w_down,
    b_down,
):
    _, local_len, width = tokens.shape
    length = n_seq * local_len
    own = w_qkv.shape[0]
    head_width = width // n_seq
    n_all = n_seq * n_batch
    me = lax.axis_index("seq")
    tokens = tokens.reshape(local_len, width)
    cotangent = cotangent.reshape(local_len, width)

    small_parts = (ln1_gain, ln1_bias, b_qv, b_out, ln2_gain, ln2_bias, b_up, b_down)
    sizes = [part.shape[0] for part in small_parts]
    n_small = sum(sizes)
    tiles = exit_mask.shape[1]
    part_width = 3 * head_width
    small = jnp.concatenate(small_parts + (exit_mask.reshape(-1).astype(LOW),))
    lanes = -(-small.shape[0] // own)
    small = jnp.pad(small, (0, own * lanes - small.shape[0])).reshape(own, lanes)
    small = jnp.pad(small, ((0, 0), (0, EXTRA - lanes)))

    by_head = w_qkv.reshape(own, 3, n_seq, head_width).transpose(2, 0, 1, 3)
    by_head = by_head.reshape(n_seq, own, part_width)
    moved = exchange(
        [
            jnp.concatenate([lax.dynamic_index_in_dim(by_head, me ^ bit, 0, False), small], axis=1)
            for bit in range(n_seq)
        ],
        n_seq,
    )
    moved = jnp.concatenate(moved, axis=0).reshape(n_seq, own, part_width + EXTRA)
    out_part = lax.all_gather(w_out, "batch", axis=0, tiled=True)
    joined = lax.all_gather(moved.reshape(n_seq * own, part_width + EXTRA), "batch", axis=0)
    up_all = lax.all_gather(w_up, "batch", axis=0, tiled=True)
    down_all = lax.all_gather(w_down, "batch", axis=0, tiled=True)
    hidden_count = up_all.shape[0]

    def unpack(extra):
        return extra[..., :lanes].reshape(extra.shape[:-2] + (own * lanes,))

    mask_row = unpack(moved[..., part_width:])[:, n_small : n_small + tiles]
    active_row = jnp.repeat(mask_row.reshape(-1), TILE).astype(WIDE).reshape(length, 1)
    joined = joined.reshape(n_batch, n_seq, own, part_width + EXTRA)
    qkv_full, small_all = assemble(me.reshape(1), joined, part_width)
    small_all = unpack(small_all.reshape(n_seq, n_batch, own, EXTRA)).astype(WIDE)
    params, at = [], 0
    for size in sizes:
        params.append(small_all[:, :, at : at + size].reshape(-1))
        at += size
    gain_one, bias_one, qv_bias, out_bias, gain_two, bias_two, up_bias_all, down_bias = params
    up_bias = lax.dynamic_slice_in_dim(up_bias_all, me * hidden_count, hidden_count)

    held_row = gather_start(tokens, n_seq)
    *held_row, out_part = tie(*gather_end(held_row, n_seq), out_part)
    row_low = jnp.concatenate(held_row, axis=0)
    out_full = jnp.concatenate(gather_shared(out_part, n_seq, n_batch), axis=0)
    active = jnp.repeat(exit_mask.reshape(-1), TILE).astype(WIDE).reshape(local_len, 1)
    grad_low = (cotangent.astype(WIDE) * active).astype(LOW)
    row_low, out_full, grad_low = tie(row_low, out_full, grad_low)
    held_grad = gather_start(grad_low, n_seq)
    row = row_low.astype(WIDE)
    centre_one, inverse_one = norm_stats(row)
    normed_one = (row - centre_one) * inverse_one
    normed_low = (normed_one * gain_one + bias_one).astype(LOW)
    normed_low, *held_grad = tie(normed_low, *held_grad)
    own_q = lax.dynamic_slice_in_dim(qv_bias, me * head_width, head_width)
    own_v = lax.dynamic_slice_in_dim(qv_bias, width + me * head_width, head_width)
    own_bias = jnp.concatenate([own_q, jnp.zeros_like(own_q), own_v])
    qkv = (product(normed_low, qkv_full) + own_bias).astype(LOW)
    qkv, *held_grad = tie(qkv, *gather_end(held_grad, n_seq))
    grad_row = jnp.concatenate(held_grad, axis=0)
    segment_row = segment_ids.reshape(length)
    starts = jnp.sum(
        (segment_row[None, :] < segment_row[:, None]).astype(jnp.int32), axis=1
    ).reshape(1, length)
    mixed, logsum = attend(me.reshape(1), qkv, starts, head_width)
    mixed_all = gather_end(gather_start(mixed, n_seq), n_seq)
    side = lax.axis_index("batch") & 1
    normed_halves = normed_low.reshape(length, n_seq, n_batch // 2, 2, own).transpose(3, 0, 2, 1, 4)
    normed_halves = normed_halves.reshape(2, length, width // 2)
    normed_sent = lax.dynamic_index_in_dim(normed_halves, 1 - side, 0, False)
    normed_kept = lax.dynamic_index_in_dim(normed_halves, side, 0, False)
    mixed_sent, mixed_kept = pair_split(mixed, n_batch)
    normed_two_low, middle_own, normed_own, inverse_own = out_norm(
        mixed_all, out_full, row_low, active_row, out_bias, gain_two, bias_two, n_seq
    )

    hidden_low, slope = ffn_up(normed_two_low, up_all, up_bias)
    grad_down_part = pair_rows(hidden_low, grad_row, n_batch)
    grad_down_part, down_all, normed_sent, normed_kept, mixed_sent, mixed_kept = tie(
        grad_down_part, down_all, normed_sent, normed_kept, mixed_sent, mixed_kept
    )
    grad_down = scatter_batch(grad_down_part, n_batch)
    d_before, grad_upb, *blocks = ffn_back(grad_row, slope, down_all, up_all, n_seq)
    parts = scatter_send(blocks, n_seq)
    grad_up_part = pair_rows(d_before, normed_two_low, n_batch)
    feed_part = product(hidden_low, down_all).astype(LOW)
    parts[0][0], grad_up_part, feed_part, grad_down = tie(
        parts[0][0], grad_up_part, feed_part, grad_down
    )
    grad_up = scatter_batch(grad_up_part, n_batch)
    grad_downb = jnp.sum(grad_low.astype(WIDE), axis=0)

    d_middle, d_branch, d_mixed, sums = norm_back(
        parts, cotangent, normed_own, inverse_own, active, gain_two, out_full, n_seq
    )
    d_mixed = jnp.concatenate(exchange([d_mixed[bit] for bit in range(n_seq)], n_seq), axis=0)
    d_mixed, d_branch, feed_part = tie(d_mixed, d_branch, feed_part)
    held_branch = gather_start(d_branch, n_seq)
    d_qkv = attend_back(me.reshape(1), qkv, d_mixed, starts, logsum, head_width)
    d_qkv, *held_branch = tie(d_qkv, *held_branch)
    d_branch_row = jnp.concatenate(gather_end(held_branch, n_seq), axis=0)

    grad_qkv_part = pair_product(normed_sent, normed_kept, d_qkv, n_batch)
    grad_qkv_part, grad_up = tie(grad_qkv_part, grad_up)
    reduced = scatter_batch(grad_qkv_part, n_batch)

    d_normed_part = product_t(d_qkv, qkv_full)
    grad_gain_one = jnp.sum(d_normed_part * normed_one, axis=0)
    grad_bias_one = jnp.sum(d_normed_part, axis=0)
    feed = scatter_end(scatter_send(scatter_split(feed_part, n_seq), n_seq)) + down_bias
    layer_out = (middle_own + active * feed).astype(LOW)
    d_normed_low, layer_out = tie(d_normed_part.astype(LOW), layer_out)

    def place(values, total):
        return lax.dynamic_update_slice_in_dim(
            jnp.zeros((total,), WIDE), values, me * values.shape[0], 0
        )

    d_bias = jnp.sum(d_qkv.astype(WIDE), axis=0)
    grad_qvb = jnp.concatenate(
        [place(d_bias[:head_width], width), place(d_bias[2 * head_width :], width)]
    )
    small_grads = (
        grad_gain_one,
        grad_bias_one,
        grad_qvb,
        sums[2],
        sums[0],
        sums[1],
        place(grad_upb.reshape(-1), n_seq * hidden_count),
        grad_downb,
    )
    packed = jnp.concatenate([g.reshape(n_seq, n_batch, -1) for g in small_grads], axis=2)
    packed = packed.transpose(1, 0, 2).reshape(n_batch, own, -1).astype(LOW)
    lanes_back = packed.shape[2]
    packed = jnp.pad(packed, ((0, 0), (0, 0), (0, EXTRA - lanes_back)))
    packed = packed.reshape(n_batch // 2, 2, own, EXTRA)
    packed_sent = lax.dynamic_index_in_dim(packed, 1 - side, 1, False).reshape(-1, EXTRA)
    packed_kept = lax.dynamic_index_in_dim(packed, side, 1, False).reshape(-1, EXTRA)
    packed_part = packed_kept + flip(packed_sent, "batch", 1, n_batch)
    grad_out_part = pair_product(mixed_sent, mixed_kept, d_branch_row, n_batch)
    grad_out_part = jnp.concatenate([grad_out_part, packed_part], axis=1)
    d_normed_one = scatter_end(scatter_send(scatter_split(d_normed_low, n_seq), n_seq))
    row_own = tokens.astype(WIDE)
    centre_own, inverse_first = norm_stats(row_own)
    d_input = d_middle + norm_backward(
        d_normed_one, (row_own - centre_own) * inverse_first, inverse_first, gain_one
    )

    grad_out_part, reduced = tie(grad_out_part, reduced)
    reduced_out = scatter_batch(grad_out_part, n_batch)
    blocks = [
        flip(lax.dynamic_slice_in_dim(reduced, (me ^ bit) * own, own, 0), "seq", bit, n_seq)
        if bit
        else lax.dynamic_slice_in_dim(reduced, me * own, own, 0)
        for bit in range(n_seq)
    ]
    grad_qkv = format_qkv(me.reshape(1), blocks, width, n_seq)
    grad_out = reduced_out[:, :width]
    small_rows = reduced_out[:, width:].reshape(n_seq, own // n_seq, EXTRA)
    small_blocks = [lax.dynamic_index_in_dim(small_rows, me ^ bit, 0, False) for bit in range(n_seq)]
    small_out = exchange(small_blocks, n_seq)
    small_out = scatter_end([[block] for block in small_out])[:, :lanes_back].reshape(-1)
    small_result, at = [], 0
    for size in sizes:
        small_result.append(small_out[at : at + size])
        at += size
    g_one, c_one, g_qvb, g_outb, g_two, c_two, g_upb, g_downb = small_result
    return (
        layer_out[None],
        d_input[None],
        g_one,
        c_one,
        grad_qkv,
        g_qvb,
        grad_out.astype(WIDE),
        g_outb,
        g_two,
        c_two,
        grad_up.astype(WIDE),
        g_upb,
        grad_down.astype(WIDE),
        g_downb,
    )


def solution(mesh):
    vector = P(("seq", "batch"))
    matrix = P(("seq", "batch"), None)
    rows = P("batch", "seq", None)
    return jax.shard_map(
        functools.partial(shards, mesh.shape["seq"], mesh.shape["batch"]),
        mesh=mesh,
        in_specs=(
            rows, rows, P("batch", None), P("batch", "seq"),
            vector, vector, matrix, vector, matrix, vector, vector, vector, matrix, vector, matrix, vector,
        ),
        out_specs=(
            rows, rows, vector, vector, matrix, vector, matrix, vector, vector, vector, matrix, vector, matrix, vector,
        ),
        check_vma=False,
    )
```

```python
import functools

import jax
import jax.numpy as jnp
from jax import lax
from jax.experimental import pallas as pl
from jax.experimental.pallas import tpu as pltpu
from jax.sharding import PartitionSpec as P

HEADS = 32
HEAD_DIM = 64
TILE = 128
PAIR = 2 * HEAD_DIM
Q_BLOCK = 256
FFN_ROWS = 512
EXTRA = 128
EPSILON = 1e-05
GELU_C = 0.7978845608028654
GELU_K = 0.044715
NEGATIVE = -1e30
VMEM_LIMIT = 56 * 1024 * 1024
LOW = jnp.bfloat16
WIDE = jnp.float32


def cost(microseconds):
    return pl.CostEstimate(flops=int(microseconds * 0.4 * 1.15e9), bytes_accessed=1 << 10, transcendentals=0)


def product(left, right):
    return jnp.dot(left, right, preferred_element_type=WIDE)


def product_t(left, right):
    return lax.dot_general(left, right, (((1,), (1,)), ((), ())), preferred_element_type=WIDE)


def product_rows(left, right):
    return lax.dot_general(left, right, (((0,), (0,)), ((), ())), preferred_element_type=WIDE)


def norm_stats(values):
    centre = jnp.mean(values, axis=-1, keepdims=True)
    centred = values - centre
    spread = jnp.mean(centred * centred, axis=-1, keepdims=True)
    return centre, lax.rsqrt(spread + EPSILON)


def norm_backward(upstream, normed, inverse, gain):
    graded = upstream * gain
    first = jnp.mean(graded, axis=-1, keepdims=True)
    second = jnp.mean(graded * normed, axis=-1, keepdims=True)
    return inverse * (graded - first - normed * second)


def flip(values, axis, bit, size):
    return lax.ppermute(values, axis, [(i, i ^ bit) for i in range(size)])


def tie(*values):
    return lax.optimization_barrier(values)


def gather_start(values, n_seq):
    if n_seq != 4:
        return [values] + [flip(values, "seq", bit, n_seq) for bit in range(1, n_seq)]
    return [values, flip(values, "seq", 1, 4), flip(values, "seq", 2, 4)]


def gather_end(held, n_seq):
    if n_seq != 4:
        return held
    values, one, two = held
    half = values.shape[0] // 2
    low = flip(one[:half], "seq", 2, 4)
    high = flip(two[half:], "seq", 1, 4)
    return [values, one, two, jnp.concatenate([low, high], axis=0)]


def exchange(blocks, n_seq):
    return [blocks[0]] + [flip(blocks[bit], "seq", bit, n_seq) for bit in range(1, n_seq)]


def scatter_start(blocks, n_seq):
    if n_seq != 4:
        return exchange(blocks, n_seq)
    own, first, second, then_second, then_first = blocks
    return [own, flip(first, "seq", 1, 4), flip(second, "seq", 2, 4), then_second, then_first]


def scatter_next(blocks, n_seq):
    if n_seq != 4:
        return [[block] for block in blocks]
    own, first, second, then_second, then_first = blocks
    half = own.shape[0] // 2
    then_second = (then_second.astype(WIDE) + first[half:].astype(WIDE)).astype(LOW)
    then_first = (then_first.astype(WIDE) + second[half:].astype(WIDE)).astype(LOW)
    then_second, then_first = flip(then_second, "seq", 2, 4), flip(then_first, "seq", 1, 4)
    return [[own], [first, second], [then_second, then_first]]


def scatter_send(blocks, n_seq):
    return scatter_next(scatter_start(blocks, n_seq), n_seq)


def scatter_end(parts):
    count = parts[0][0].shape[0]
    total = parts[0][0].astype(WIDE)
    for part in parts[1:]:
        rows = count // len(part)
        total = total + jnp.concatenate([piece[:rows] for piece in part], axis=0).astype(WIDE)
    return total


def pair_split(left, n_batch):
    side = lax.axis_index("batch") & 1
    blocks = left.reshape(left.shape[0], n_batch // 2, 2, left.shape[1] // n_batch)
    sent = lax.dynamic_index_in_dim(blocks, 1 - side, 2, False)
    kept = lax.dynamic_index_in_dim(blocks, side, 2, False)
    return sent.reshape(left.shape[0], -1), kept.reshape(left.shape[0], -1)


def rows_kernel(side_ref, left_ref, right_ref, *refs):
    total = product_rows(left_ref[...], right_ref[...])
    if len(refs) == 2:
        total += refs[0][...].astype(WIDE)
    refs[-1][...] = total.astype(LOW)


def rows_product(side, left, right, added, n_batch):
    length, columns = left.shape
    width = right.shape[1]
    count = columns // n_batch
    block = pl.BlockSpec((count, width), lambda k, side: (k, 0))
    return pl.pallas_call(
        rows_kernel,
        grid_spec=pltpu.PrefetchScalarGridSpec(
            num_scalar_prefetch=1,
            grid=(n_batch // 2,),
            in_specs=[
                pl.BlockSpec((length, count), lambda k, side: (0, 2 * k + side[0])),
                pl.BlockSpec((length, width), lambda k, side: (0, 0), pipeline_mode=pl.Buffered(1)),
            ]
            + [block] * len(added),
            out_specs=block,
        ),
        out_shape=jax.ShapeDtypeStruct((columns // 2, width), LOW),
        compiler_params=pltpu.CompilerParams(vmem_limit_bytes=VMEM_LIMIT),
        cost_estimate=cost(9),
        name="rows_product",
    )(side, left, right, *added)


def pair_rows(left, right, n_batch):
    if left.shape[1] // n_batch % 128:
        return pair_product(*pair_split(left, n_batch), right, n_batch)
    side = (lax.axis_index("batch") & 1).reshape(1)
    moved = flip(rows_product(1 - side, left, right, (), n_batch), "batch", 1, n_batch)
    return rows_product(side, left, right, (moved,), n_batch)


def pair_product(sent, kept, right, n_batch):
    moved = flip(product_rows(sent, right).astype(LOW), "batch", 1, n_batch)
    return (product_rows(kept, right) + moved.astype(WIDE)).astype(LOW)


def scatter_batch(total, n_batch):
    groups = [list(range(0, n_batch, 2)), list(range(1, n_batch, 2))]
    return lax.psum_scatter(
        total,
        "batch",
        scatter_dimension=0,
        tiled=True,
        axis_index_groups=groups,
    )


def key_range(q_start, q_count, length):
    low = max(0, (q_start - (length // 2 - 1)) // q_count * q_count)
    return low, q_start + q_count


def block_mask(starts, low, high, q_start, q_count):
    shape = (high - low, q_count)
    key = low + lax.broadcasted_iota(jnp.int32, shape, 0)
    query = q_start + lax.broadcasted_iota(jnp.int32, shape, 1)
    return (key <= query) & (key >= starts)


def load_natural(me, pairs):
    for source, target in pairs:
        for block in range(target.shape[0] // Q_BLOCK):
            at = pl.multiple_of((block ^ me) * Q_BLOCK, Q_BLOCK)
            target[block * Q_BLOCK : (block + 1) * Q_BLOCK, :] = source[pl.ds(at, Q_BLOCK), :]


def attend_kernel(me_ref, q_ref, k_ref, v_ref, start_ref, o_ref, lse_ref, k_own, v_own):
    length = q_ref.shape[0]
    me = me_ref[0]
    load_natural(me, ((k_ref, k_own), (v_ref, v_own)))
    lane = lax.broadcasted_iota(jnp.int32, (1, PAIR), 1)
    row = lax.broadcasted_iota(jnp.int32, (PAIR, 1), 0)
    for q_start in range(0, length, Q_BLOCK):
        low, high = key_range(q_start, Q_BLOCK, length)
        here = slice(q_start, q_start + Q_BLOCK)
        there = pl.ds(pl.multiple_of((q_start // Q_BLOCK ^ me) * Q_BLOCK, Q_BLOCK), Q_BLOCK)
        q, k, v = q_ref[there, :], k_own[low:high, :], v_own[low:high, :]
        allowed = block_mask(start_ref[:, here], low, high, q_start, Q_BLOCK)
        mixed = []
        for head in range(2):
            mine = (lane >= head * HEAD_DIM) & (lane < (head + 1) * HEAD_DIM)
            q_head = jnp.where(mine, q, jnp.zeros_like(q))
            scores = product_t(k, q_head) * HEAD_DIM ** (-0.5)
            scores = jnp.where(allowed, scores, NEGATIVE)
            peak = jnp.max(scores, axis=0, keepdims=True)
            raised = jnp.exp(scores - peak)
            total = jnp.sum(raised, axis=0, keepdims=True)
            probs = (raised / total).astype(LOW)
            mixed.append(product_rows(v, probs))
            lse_ref[0, head : head + 1, here] = peak + jnp.log(total)
        joined = jnp.where(row < HEAD_DIM, mixed[0], mixed[1])
        o_ref[there, :] = joined.T.astype(LOW)


def attend(me, qkv, starts, width):
    length = qkv.shape[0]
    pairs = width // PAIR
    return pl.pallas_call(
        attend_kernel,
        grid_spec=pltpu.PrefetchScalarGridSpec(
            num_scalar_prefetch=1,
            grid=(pairs,),
            in_specs=[
                pl.BlockSpec((length, PAIR), lambda j, me: (0, j)),
                pl.BlockSpec((length, PAIR), lambda j, me: (0, pairs + j)),
                pl.BlockSpec((length, PAIR), lambda j, me: (0, 2 * pairs + j)),
                pl.BlockSpec((1, length), lambda j, me: (0, 0)),
            ],
            out_specs=[
                pl.BlockSpec((length, PAIR), lambda j, me: (0, j)),
                pl.BlockSpec((1, 2, length), lambda j, me: (j, 0, 0)),
            ],
            scratch_shapes=[pltpu.VMEM((length, PAIR), LOW), pltpu.VMEM((length, PAIR), LOW)],
        ),
        out_shape=[
            jax.ShapeDtypeStruct((length, width), LOW),
            jax.ShapeDtypeStruct((pairs, 2, length), WIDE),
        ],
        compiler_params=pltpu.CompilerParams(vmem_limit_bytes=VMEM_LIMIT),
        cost_estimate=cost(20.5),
        name="attend",
    )(me, qkv, qkv, qkv, starts)


def attend_back_kernel(
    me_ref, q_ref, k_ref, v_ref, do_ref, start_ref, lse_ref, out_ref, k_own, v_own, dk_acc, dv_acc
):
    length = q_ref.shape[0]
    width = out_ref.shape[1] // 3
    me = me_ref[0]
    at = pl.program_id(0) * PAIR
    scale = HEAD_DIM ** (-0.5)
    lane = lax.broadcasted_iota(jnp.int32, (1, PAIR), 1)
    row = lax.broadcasted_iota(jnp.int32, (PAIR, 1), 0)
    load_natural(me, ((k_ref, k_own), (v_ref, v_own)))
    dk_acc[...] = jnp.zeros_like(dk_acc)
    dv_acc[...] = jnp.zeros_like(dv_acc)
    for q_start in range(0, length, Q_BLOCK):
        low, high = key_range(q_start, Q_BLOCK, length)
        here = slice(q_start, q_start + Q_BLOCK)
        there = pl.ds(pl.multiple_of((q_start // Q_BLOCK ^ me) * Q_BLOCK, Q_BLOCK), Q_BLOCK)
        q, k, v, do = q_ref[there, :], k_own[low:high, :], v_own[low:high, :], do_ref[there, :]
        allowed = block_mask(start_ref[:, here], low, high, q_start, Q_BLOCK)
        d_query = []
        for head in range(2):
            mine = (lane >= head * HEAD_DIM) & (lane < (head + 1) * HEAD_DIM)
            q_head = jnp.where(mine, q, jnp.zeros_like(q))
            do_head = jnp.where(mine, do, jnp.zeros_like(do))
            scores = product_t(k, q_head) * scale - lse_ref[0, head : head + 1, here]
            probs = jnp.exp(jnp.where(allowed, scores, NEGATIVE))
            d_probs = product_t(v, do_head)
            delta = jnp.sum(probs * d_probs, axis=0, keepdims=True)
            d_scores = (probs * (d_probs - delta)).astype(LOW)
            d_query.append(product_rows(k, d_scores))
            dk_acc[low:high, :] += product(d_scores, q_head)
            dv_acc[low:high, :] += product(probs.astype(LOW), do_head)
        joined = jnp.where(row < HEAD_DIM, d_query[0], d_query[1]) * scale
        out_ref[there, pl.ds(pl.multiple_of(at, PAIR), PAIR)] = joined.T.astype(LOW)
    for q_start in range(0, length, Q_BLOCK):
        here = slice(q_start, q_start + Q_BLOCK)
        there = pl.ds(pl.multiple_of((q_start // Q_BLOCK ^ me) * Q_BLOCK, Q_BLOCK), Q_BLOCK)
        d_key = (dk_acc[here, :] * scale).astype(LOW)
        out_ref[there, pl.ds(pl.multiple_of(width + at, PAIR), PAIR)] = d_key
        d_value = dv_acc[here, :].astype(LOW)
        out_ref[there, pl.ds(pl.multiple_of(2 * width + at, PAIR), PAIR)] = d_value


def attend_back(me, qkv, d_mixed, starts, logsum, width):
    length = qkv.shape[0]
    pairs = width // PAIR
    return pl.pallas_call(
        attend_back_kernel,
        grid_spec=pltpu.PrefetchScalarGridSpec(
            num_scalar_prefetch=1,
            grid=(pairs,),
            in_specs=[
                pl.BlockSpec((length, PAIR), lambda j, me: (0, j)),
                pl.BlockSpec((length, PAIR), lambda j, me: (0, pairs + j)),
                pl.BlockSpec((length, PAIR), lambda j, me: (0, 2 * pairs + j)),
                pl.BlockSpec((length, PAIR), lambda j, me: (0, j)),
                pl.BlockSpec((1, length), lambda j, me: (0, 0)),
                pl.BlockSpec((1, 2, length), lambda j, me: (j, 0, 0)),
            ],
            out_specs=pl.BlockSpec((length, 3 * width), lambda j, me: (0, 0)),
            scratch_shapes=[
                pltpu.VMEM((length, PAIR), LOW),
                pltpu.VMEM((length, PAIR), LOW),
                pltpu.VMEM((length, PAIR), WIDE),
                pltpu.VMEM((length, PAIR), WIDE),
            ],
        ),
        out_shape=jax.ShapeDtypeStruct((length, 3 * width), LOW),
        compiler_params=pltpu.CompilerParams(vmem_limit_bytes=VMEM_LIMIT),
        cost_estimate=cost(23.4),
        name="attend_back",
    )(me, qkv, qkv, qkv, d_mixed, starts, logsum)


def out_norm_kernel(n_seq, *refs):
    o_refs = refs[:n_seq]
    w_ref, row_ref, active_ref, bias_ref, gain_ref, shift_ref = refs[n_seq : n_seq + 6]
    low_ref, middle_ref, normed_ref, inverse_ref = refs[n_seq + 6 :]
    depth = o_refs[0].shape[1]
    branch = product(o_refs[0][...], w_ref[:depth, :])
    for block in range(1, n_seq):
        branch += product(o_refs[block][...], w_ref[block * depth : (block + 1) * depth, :])
    middle = row_ref[...].astype(WIDE) + active_ref[...] * (branch + bias_ref[...])
    centre, inverse = norm_stats(middle)
    normed = (middle - centre) * inverse
    low_ref[...] = (normed * gain_ref[...] + shift_ref[...]).astype(LOW)

    @pl.when(pl.program_id(0) == 0)
    def _():
        middle_ref[...] = middle
        normed_ref[...] = normed
        inverse_ref[...] = inverse


def out_norm(mixed_all, out_full, row_low, active_row, bias, gain, shift, n_seq):
    length, width = row_low.shape
    count = length // n_seq
    depth = width // n_seq

    def mixed_spec(bit):
        return pl.BlockSpec((count, depth), lambda k: (k ^ bit, 0))

    vector = pl.BlockSpec((1, width), lambda k: (0, 0))
    block = pl.BlockSpec((count, width), lambda k: (k, 0))
    first = pl.BlockSpec((count, width), lambda k: (0, 0))
    return pl.pallas_call(
        functools.partial(out_norm_kernel, n_seq),
        grid=(n_seq,),
        in_specs=[mixed_spec(bit) for bit in range(n_seq)]
        + [
            pl.BlockSpec((width, width), lambda k: (0, 0)),
            block,
            pl.BlockSpec((count, 1), lambda k: (k, 0)),
            vector,
            vector,
            vector,
        ],
        out_specs=[block, first, first, pl.BlockSpec((count, 1), lambda k: (0, 0))],
        out_shape=[
            jax.ShapeDtypeStruct((length, width), LOW),
            jax.ShapeDtypeStruct((count, width), WIDE),
            jax.ShapeDtypeStruct((count, width), WIDE),
            jax.ShapeDtypeStruct((count, 1), WIDE),
        ],
        compiler_params=pltpu.CompilerParams(vmem_limit_bytes=VMEM_LIMIT),
        cost_estimate=cost(19.4),
        name="out_norm",
    )(
        *mixed_all,
        out_full,
        row_low,
        active_row,
        bias.reshape(1, width),
        gain.reshape(1, width),
        shift.reshape(1, width),
    )


def assemble_kernel(me_ref, joined_ref, full_ref, extra_ref):
    own = joined_ref.shape[2]
    width = full_ref.shape[1]
    for member in range(joined_ref.shape[0]):
        rows = slice(member * own, (member + 1) * own)
        full_ref[rows, :] = joined_ref[member, 0, :, :width]
        extra_ref[rows, :] = joined_ref[member, 0, :, width:]


def assemble(me, joined, width):
    n_batch, n_seq, own, columns = joined.shape
    count = n_batch * own
    return pl.pallas_call(
        assemble_kernel,
        grid_spec=pltpu.PrefetchScalarGridSpec(
            num_scalar_prefetch=1,
            grid=(n_seq,),
            in_specs=[
                pl.BlockSpec((n_batch, 1, own, columns), lambda j, me: (0, j ^ me[0], 0, 0)),
            ],
            out_specs=[
                pl.BlockSpec((count, width), lambda j, me: (j, 0)),
                pl.BlockSpec((count, EXTRA), lambda j, me: (j, 0)),
            ],
        ),
        out_shape=[
            jax.ShapeDtypeStruct((n_seq * count, width), LOW),
            jax.ShapeDtypeStruct((n_seq * count, EXTRA), LOW),
        ],
        compiler_params=pltpu.CompilerParams(vmem_limit_bytes=VMEM_LIMIT),
        cost_estimate=cost(6.2),
        name="assemble",
    )(me, joined)


def ffn_up_kernel(n_ref, w_ref, bias_ref, hidden_ref, slope_ref):
    step = 512
    for at in range(0, w_ref.shape[0], step):
        here = slice(at, at + step)
        before = product_t(n_ref[...], w_ref[here, :]) + bias_ref[:, here]
        square = before * before
        tangent = jnp.tanh(before * (GELU_C + GELU_C * GELU_K * square))
        half = 0.5 + 0.5 * tangent
        hidden = before * half
        hidden_ref[:, here] = hidden.astype(LOW)
        slope_ref[:, here] = half + hidden * (1.0 - tangent) * (
            GELU_C + 3.0 * GELU_C * GELU_K * square
        )


def ffn_up(normed, w_up, bias):
    length, width = normed.shape
    hidden = w_up.shape[0]
    return pl.pallas_call(
        ffn_up_kernel,
        grid=(length // FFN_ROWS,),
        in_specs=[
            pl.BlockSpec((FFN_ROWS, width), lambda k: (k, 0)),
            pl.BlockSpec((hidden, width), lambda k: (0, 0), pipeline_mode=pl.Buffered(1)),
            pl.BlockSpec((1, hidden), lambda k: (0, 0)),
        ],
        out_specs=[
            pl.BlockSpec((FFN_ROWS, hidden), lambda k: (k, 0)),
            pl.BlockSpec((FFN_ROWS, hidden), lambda k: (k, 0)),
        ],
        out_shape=[
            jax.ShapeDtypeStruct((length, hidden), LOW),
            jax.ShapeDtypeStruct((length, hidden), WIDE),
        ],
        compiler_params=pltpu.CompilerParams(vmem_limit_bytes=VMEM_LIMIT),
        cost_estimate=cost(19.6),
        name="ffn_up",
    )(normed, w_up, bias.reshape(1, hidden))


def split_sizes(count, n_seq):
    return [count] * n_seq if n_seq != 4 else [count, count, count, count // 2, count // 2]


def split_specs(count, width, n_seq):
    return [pl.BlockSpec((size, width), lambda k: (0, 0)) for size in split_sizes(count, n_seq)]


def split_shapes(count, width, n_seq):
    return [jax.ShapeDtypeStruct((size, width), LOW) for size in split_sizes(count, n_seq)]


def split_store(index, values, outs, n_seq):
    half = values.shape[0] // 2
    if n_seq != 4:
        places = [[(outs[bit], 0, slice(None))] for bit in range(n_seq)]
    else:
        own, first, second, then_second, then_first = outs
        upper, lower = slice(0, half), slice(half, 2 * half)
        places = [
            [(own, 0, slice(None))],
            [(first, 0, upper), (then_first, 0, lower)],
            [(then_second, 0, upper), (second, 0, lower)],
            [(first, half, upper), (second, half, lower)],
        ]
    for bit, targets in enumerate(places):

        @pl.when(index == bit)
        def _():
            for target, at, rows in targets:
                piece = values[rows]
                target[at : at + piece.shape[0], :] = piece


def ffn_back_kernel(n_seq, grad_ref, slope_ref, down_ref, up_ref, d_before_ref, sum_ref, *refs):
    outs, (down, up, sems) = refs[:-3], refs[-3:]
    index = pl.program_id(0)
    load_down = pltpu.make_async_copy(down_ref, down, sems.at[0])
    load_up = pltpu.make_async_copy(up_ref, up, sems.at[1])

    @pl.when(index == 0)
    def _():
        load_down.start()
        load_up.start()
        sum_ref[...] = jnp.zeros_like(sum_ref)
        load_down.wait()

    step = 512
    for at in range(0, down.shape[0], step):
        here = slice(at, at + step)
        d_hidden = product_t(grad_ref[...], down[here, :])
        d_before = (d_hidden * slope_ref[:, here]).astype(LOW)
        d_before_ref[:, here] = d_before
        sum_ref[:, here] += jnp.sum(d_before.astype(WIDE), axis=0, keepdims=True)

    @pl.when(index == 0)
    def _():
        load_up.wait()

    d_normed = product(d_before_ref[...], up[...]).astype(LOW)
    split_store(index, d_normed, outs, n_seq)


def ffn_back(grad_row, slope, w_down, w_up, n_seq):
    length, width = grad_row.shape
    hidden = w_up.shape[0]
    count = length // n_seq
    return pl.pallas_call(
        functools.partial(ffn_back_kernel, n_seq),
        grid=(n_seq,),
        in_specs=[
            pl.BlockSpec((count, width), lambda k: (k, 0)),
            pl.BlockSpec((count, hidden), lambda k: (k, 0)),
            pl.BlockSpec(memory_space=pl.ANY),
            pl.BlockSpec(memory_space=pl.ANY),
        ],
        out_specs=[
            pl.BlockSpec((count, hidden), lambda k: (k, 0)),
            pl.BlockSpec((1, hidden), lambda k: (0, 0)),
        ]
        + split_specs(count, width, n_seq),
        out_shape=[
            jax.ShapeDtypeStruct((length, hidden), LOW),
            jax.ShapeDtypeStruct((1, hidden), WIDE),
        ]
        + split_shapes(count, width, n_seq),
        scratch_shapes=[
            pltpu.VMEM((hidden, width), LOW),
            pltpu.VMEM((hidden, width), LOW),
            pltpu.SemaphoreType.DMA((2,)),
        ],
        compiler_params=pltpu.CompilerParams(vmem_limit_bytes=VMEM_LIMIT),
        cost_estimate=cost(28),
        name="ffn_back",
    )(grad_row, slope, w_down, w_up)


def feed_kernel(n_seq, hidden_ref, down_ref, *outs):
    values = product(hidden_ref[...], down_ref[...]).astype(LOW)
    split_store(pl.program_id(0), values, outs, n_seq)


def feed_down(hidden_low, w_down, n_seq):
    length, hidden = hidden_low.shape
    width = w_down.shape[1]
    count = length // n_seq
    return pl.pallas_call(
        functools.partial(feed_kernel, n_seq),
        grid=(n_seq,),
        in_specs=[
            pl.BlockSpec((count, hidden), lambda k: (k, 0)),
            pl.BlockSpec((hidden, width), lambda k: (0, 0), pipeline_mode=pl.Buffered(1)),
        ],
        out_specs=split_specs(count, width, n_seq),
        out_shape=split_shapes(count, width, n_seq),
        compiler_params=pltpu.CompilerParams(vmem_limit_bytes=VMEM_LIMIT),
        cost_estimate=cost(15.6),
        name="feed_down",
    )(hidden_low, w_down)


def qkv_back_kernel(n_seq, grad_ref, w_ref, row_ref, sums_ref, bias_ref, *outs):
    index = pl.program_id(0)

    @pl.when(index == 0)
    def _():
        sums_ref[...] = jnp.zeros_like(sums_ref)
        bias_ref[...] = jnp.zeros_like(bias_ref)

    d_normed = product_t(grad_ref[...], w_ref[...])
    row = row_ref[...].astype(WIDE)
    centre, inverse = norm_stats(row)
    normed = (row - centre) * inverse
    sums_ref[0:1, :] += jnp.sum(d_normed * normed, axis=0, keepdims=True)
    sums_ref[1:2, :] += jnp.sum(d_normed, axis=0, keepdims=True)
    bias_ref[0:1, :] += jnp.sum(grad_ref[...].astype(WIDE), axis=0, keepdims=True)
    split_store(index, d_normed.astype(LOW), outs, n_seq)


def qkv_back(d_qkv, qkv_full, row_low, n_seq):
    length, width = row_low.shape
    columns = d_qkv.shape[1]
    count = length // n_seq
    return pl.pallas_call(
        functools.partial(qkv_back_kernel, n_seq),
        grid=(n_seq,),
        in_specs=[
            pl.BlockSpec((count, columns), lambda k: (k, 0)),
            pl.BlockSpec((width, columns), lambda k: (0, 0), pipeline_mode=pl.Buffered(1)),
            pl.BlockSpec((count, width), lambda k: (k, 0)),
        ],
        out_specs=[
            pl.BlockSpec((8, width), lambda k: (0, 0)),
            pl.BlockSpec((8, columns), lambda k: (0, 0)),
        ]
        + split_specs(count, width, n_seq),
        out_shape=[
            jax.ShapeDtypeStruct((8, width), WIDE),
            jax.ShapeDtypeStruct((8, columns), WIDE),
        ]
        + split_shapes(count, width, n_seq),
        compiler_params=pltpu.CompilerParams(vmem_limit_bytes=VMEM_LIMIT),
        cost_estimate=cost(15.3),
        name="qkv_back",
    )(d_qkv, qkv_full, row_low)


def norm_back_kernel(pieces, *refs):
    n_parts = sum(pieces)
    parts, at = [], 0
    for number in pieces:
        parts.append(refs[at : at + number])
        at += number
    cot_ref, normed_ref, inverse_ref, active_ref, gain_ref, w_ref = refs[n_parts : n_parts + 6]
    d_middle_ref, d_branch_ref, d_mixed_ref, sums_ref = refs[n_parts + 6 :]

    @pl.when(pl.program_id(0) == 0)
    def _():
        upstream = parts[0][0][...].astype(WIDE)
        for part in parts[1:]:
            upstream += jnp.concatenate([piece[...] for piece in part], axis=0).astype(WIDE)
        normed = normed_ref[...]
        d_middle = cot_ref[...].astype(WIDE) + norm_backward(
            upstream, normed, inverse_ref[...], gain_ref[...]
        )
        d_middle_ref[...] = d_middle
        d_branch = (d_middle * active_ref[...]).astype(LOW)
        d_branch_ref[...] = d_branch
        sums_ref[...] = jnp.zeros_like(sums_ref)
        sums_ref[0:1, :] = jnp.sum(upstream * normed, axis=0, keepdims=True)
        sums_ref[1:2, :] = jnp.sum(upstream, axis=0, keepdims=True)
        sums_ref[2:3, :] = jnp.sum(d_branch.astype(WIDE), axis=0, keepdims=True)

    d_mixed_ref[0] = product_t(d_branch_ref[...], w_ref[...]).astype(LOW)


def norm_back(parts, cotangent, normed, inverse, active, gain, out_full, n_seq):
    count, width = cotangent.shape
    depth = width // n_seq
    block = pl.BlockSpec((count, width), lambda j: (0, 0))
    column = pl.BlockSpec((count, 1), lambda j: (0, 0))
    return pl.pallas_call(
        functools.partial(norm_back_kernel, [len(part) for part in parts]),
        grid=(n_seq,),
        in_specs=[
            pl.BlockSpec((count // len(part), width), lambda j: (0, 0)) for part in parts for piece in part
        ]
        + [block, block]
        + [
            column,
            column,
            pl.BlockSpec((1, width), lambda j: (0, 0)),
            pl.BlockSpec((depth, width), lambda j: (j, 0)),
        ],
        out_specs=[
            block,
            block,
            pl.BlockSpec((1, count, depth), lambda j: (j, 0, 0)),
            pl.BlockSpec((8, width), lambda j: (0, 0)),
        ],
        out_shape=[
            jax.ShapeDtypeStruct((count, width), WIDE),
            jax.ShapeDtypeStruct((count, width), LOW),
            jax.ShapeDtypeStruct((n_seq, count, depth), LOW),
            jax.ShapeDtypeStruct((8, width), WIDE),
        ],
        compiler_params=pltpu.CompilerParams(vmem_limit_bytes=VMEM_LIMIT),
        cost_estimate=cost(11),
        name="norm_back",
    )(
        *[piece for part in parts for piece in part],
        cotangent,
        normed,
        inverse,
        active,
        gain.reshape(1, width),
        out_full,
    )


def format_kernel(n_seq, me_ref, *refs):
    out_ref = refs[n_seq]
    width = out_ref.shape[1] // 3
    count = width // n_seq
    for block in range(n_seq):
        ref = refs[block]
        for kind in range(3):
            at = kind * width + (me_ref[0] ^ block) * count
            at = pl.multiple_of(at, count)
            out_ref[:, pl.ds(at, count)] = ref[:, kind * count : (kind + 1) * count].astype(WIDE)


def format_qkv(me, blocks, width, n_seq):
    own = blocks[0].shape[0]
    return pl.pallas_call(
        functools.partial(format_kernel, n_seq),
        grid_spec=pltpu.PrefetchScalarGridSpec(
            num_scalar_prefetch=1,
            grid=(1,),
            in_specs=[pl.BlockSpec(blocks[0].shape, lambda i, me: (0, 0))] * n_seq,
            out_specs=pl.BlockSpec((own, 3 * width), lambda i, me: (0, 0)),
        ),
        out_shape=jax.ShapeDtypeStruct((own, 3 * width), WIDE),
        compiler_params=pltpu.CompilerParams(vmem_limit_bytes=VMEM_LIMIT),
        cost_estimate=cost(2.5),
        name="format_qkv",
    )(me, *blocks)


def gather_shared(values, n_seq, n_batch):
    half = values.shape[0] // 2
    side = lax.axis_index("batch") & 1
    mine = lax.dynamic_slice_in_dim(values, side * half, half, 0)
    held = gather_end(gather_start(mine, n_seq), n_seq)[1:]
    other = [flip(block, "batch", 1, n_batch) for block in held]
    blocks = [values]
    for mine, theirs in zip(held, other):
        blocks.append(jnp.where(side == 0, mine, theirs))
        blocks.append(jnp.where(side == 0, theirs, mine))
    return blocks


def shards(
    n_seq,
    n_batch,
    tokens,
    cotangent,
    segment_ids,
    exit_mask,
    ln1_gain,
    ln1_bias,
    w_qkv,
    b_qv,
    w_out,
    b_out,
    ln2_gain,
    ln2_bias,
    w_up,
    b_up,
    w_down,
    b_down,
):
    _, local_len, width = tokens.shape
    length = n_seq * local_len
    own = w_qkv.shape[0]
    head_width = width // n_seq
    n_all = n_seq * n_batch
    me = lax.axis_index("seq")
    tokens = tokens.reshape(local_len, width)
    cotangent = cotangent.reshape(local_len, width)

    small_parts = (ln1_gain, ln1_bias, b_qv, b_out, ln2_gain, ln2_bias, b_up, b_down)
    sizes = [part.shape[0] for part in small_parts]
    n_small = sum(sizes)
    tiles = exit_mask.shape[1]
    part_width = 3 * head_width
    small = jnp.concatenate(small_parts + (exit_mask.reshape(-1).astype(LOW),))
    lanes = -(-small.shape[0] // own)
    small = jnp.pad(small, (0, own * lanes - small.shape[0])).reshape(own, lanes)
    small = jnp.pad(small, ((0, 0), (0, EXTRA - lanes)))

    by_head = w_qkv.reshape(own, 3, n_seq, head_width).transpose(2, 0, 1, 3)
    by_head = by_head.reshape(n_seq, own, part_width)
    moved = exchange(
        [
            jnp.concatenate([lax.dynamic_index_in_dim(by_head, me ^ bit, 0, False), small], axis=1)
            for bit in range(n_seq)
        ],
        n_seq,
    )
    held_row = gather_start(tokens, n_seq)
    tied = tie(*moved, *held_row)
    moved, held_row = list(tied[:n_seq]), list(tied[n_seq:])
    moved = jnp.concatenate(moved, axis=0).reshape(n_seq, own, part_width + EXTRA)
    out_part = lax.all_gather(w_out, "batch", axis=0, tiled=True)
    joined = lax.all_gather(moved.reshape(n_seq * own, part_width + EXTRA), "batch", axis=0)
    up_all = lax.all_gather(w_up, "batch", axis=0, tiled=True)
    down_all = lax.all_gather(w_down, "batch", axis=0, tiled=True)
    hidden_count = up_all.shape[0]

    def unpack(extra):
        return extra[..., :lanes].reshape(extra.shape[:-2] + (own * lanes,))

    mask_row = unpack(moved[..., part_width:])[:, n_small : n_small + tiles]
    active_row = jnp.repeat(mask_row.reshape(-1), TILE).astype(WIDE).reshape(length, 1)
    joined = joined.reshape(n_batch, n_seq, own, part_width + EXTRA)
    qkv_full, small_all = assemble(me.reshape(1), joined, part_width)
    small_all = unpack(small_all.reshape(n_seq, n_batch, own, EXTRA)).astype(WIDE)
    params, at = [], 0
    for size in sizes:
        params.append(small_all[:, :, at : at + size].reshape(-1))
        at += size
    gain_one, bias_one, qv_bias, out_bias, gain_two, bias_two, up_bias_all, down_bias = params
    up_bias = lax.dynamic_slice_in_dim(up_bias_all, me * hidden_count, hidden_count)

    *held_row, out_part = tie(*gather_end(held_row, n_seq), out_part)
    row_low = jnp.concatenate(held_row, axis=0)
    out_full = jnp.concatenate(gather_shared(out_part, n_seq, n_batch), axis=0)
    active = jnp.repeat(exit_mask.reshape(-1), TILE).astype(WIDE).reshape(local_len, 1)
    grad_low = (cotangent.astype(WIDE) * active).astype(LOW)
    row_low, out_full, grad_low = tie(row_low, out_full, grad_low)
    held_grad = gather_start(grad_low, n_seq)
    row = row_low.astype(WIDE)
    centre_one, inverse_one = norm_stats(row)
    normed_one = (row - centre_one) * inverse_one
    normed_low = (normed_one * gain_one + bias_one).astype(LOW)
    normed_low, *held_grad = tie(normed_low, *held_grad)
    own_q = lax.dynamic_slice_in_dim(qv_bias, me * head_width, head_width)
    own_v = lax.dynamic_slice_in_dim(qv_bias, width + me * head_width, head_width)
    own_bias = jnp.concatenate([own_q, jnp.zeros_like(own_q), own_v])
    qkv = (product(normed_low, qkv_full) + own_bias).astype(LOW)
    qkv, *held_grad = tie(qkv, *gather_end(held_grad, n_seq))
    grad_row = jnp.concatenate(held_grad, axis=0)
    segment_row = segment_ids.reshape(length)
    starts = jnp.sum(
        (segment_row[None, :] < segment_row[:, None]).astype(jnp.int32), axis=1
    ).reshape(1, length)
    mixed, logsum = attend(me.reshape(1), qkv, starts, head_width)
    mixed_all = gather_end(gather_start(mixed, n_seq), n_seq)
    side = lax.axis_index("batch") & 1
    normed_halves = normed_low.reshape(length, n_seq, n_batch // 2, 2, own).transpose(3, 0, 2, 1, 4)
    normed_halves = normed_halves.reshape(2, length, width // 2)
    normed_sent = lax.dynamic_index_in_dim(normed_halves, 1 - side, 0, False)
    normed_kept = lax.dynamic_index_in_dim(normed_halves, side, 0, False)
    mixed_sent, mixed_kept = pair_split(mixed, n_batch)
    normed_two_low, middle_own, normed_own, inverse_own = out_norm(
        mixed_all, out_full, row_low, active_row, out_bias, gain_two, bias_two, n_seq
    )

    hidden_low, slope = ffn_up(normed_two_low, up_all, up_bias)
    grad_down_part = pair_rows(hidden_low, grad_row, n_batch)
    grad_down_part, down_all, normed_sent, normed_kept, mixed_sent, mixed_kept = tie(
        grad_down_part, down_all, normed_sent, normed_kept, mixed_sent, mixed_kept
    )
    grad_down = scatter_batch(grad_down_part, n_batch)
    d_before, grad_upb, *blocks = ffn_back(grad_row, slope, down_all, up_all, n_seq)
    parts = scatter_send(blocks, n_seq)
    grad_up_part = pair_rows(d_before, normed_two_low, n_batch)
    feed_blocks = feed_down(hidden_low, down_all, n_seq)
    parts[0][0], grad_up_part, *feed_blocks = tie(parts[0][0], grad_up_part, *feed_blocks)
    grad_up = scatter_batch(grad_up_part, n_batch)
    grad_downb = jnp.sum(grad_low.astype(WIDE), axis=0)

    d_middle, d_branch, d_mixed, sums = norm_back(
        parts, cotangent, normed_own, inverse_own, active, gain_two, out_full, n_seq
    )
    d_mixed = jnp.concatenate(exchange([d_mixed[bit] for bit in range(n_seq)], n_seq), axis=0)
    d_mixed, d_branch = tie(d_mixed, d_branch)
    held_branch = gather_start(d_branch, n_seq)
    d_qkv = attend_back(me.reshape(1), qkv, d_mixed, starts, logsum, head_width)
    tied = tie(d_qkv, *held_branch, *feed_blocks)
    d_qkv, held_branch, feed_blocks = tied[0], tied[1 : len(held_branch) + 1], tied[len(held_branch) + 1 :]
    d_branch_row = jnp.concatenate(gather_end(held_branch, n_seq), axis=0)

    grad_qkv_part = pair_product(normed_sent, normed_kept, d_qkv, n_batch)
    grad_qkv_part, grad_up, grad_down = tie(grad_qkv_part, grad_up, grad_down)
    reduced = scatter_batch(grad_qkv_part, n_batch)

    sums_one, d_bias, *blocks_one = qkv_back(d_qkv, qkv_full, row_low, n_seq)
    d_bias = d_bias[0]
    tied = tie(*scatter_start(blocks_one, n_seq), *feed_blocks)
    blocks_one, feed_blocks = tied[: len(blocks_one)], scatter_start(tied[len(blocks_one) :], n_seq)

    def place(values, total):
        return lax.dynamic_update_slice_in_dim(
            jnp.zeros((total,), WIDE), values, me * values.shape[0], 0
        )

    grad_qvb = jnp.concatenate(
        [place(d_bias[:head_width], width), place(d_bias[2 * head_width :], width)]
    )
    small_grads = (
        sums_one[0],
        sums_one[1],
        grad_qvb,
        sums[2],
        sums[0],
        sums[1],
        place(grad_upb.reshape(-1), n_seq * hidden_count),
        grad_downb,
    )
    packed = jnp.concatenate([g.reshape(n_seq, n_batch, -1) for g in small_grads], axis=2)
    rows_back = -(-n_small // EXTRA)
    packed = jnp.pad(packed, ((0, 0), (0, 0), (0, rows_back * EXTRA - n_small)))
    packed = packed.reshape(n_seq, n_batch, rows_back, EXTRA).transpose(1, 0, 2, 3).astype(LOW)
    packed = packed.reshape(n_batch // 2, 2, n_seq * rows_back, EXTRA)
    packed = jnp.pad(packed, ((0, 0), (0, 0), (0, own - n_seq * rows_back), (0, 0)))
    packed_sent = lax.dynamic_index_in_dim(packed, 1 - side, 1, False).reshape(-1, EXTRA)
    packed_kept = lax.dynamic_index_in_dim(packed, side, 1, False).reshape(-1, EXTRA)
    packed_part = packed_kept + flip(packed_sent, "batch", 1, n_batch)
    grad_out_part = pair_product(mixed_sent, mixed_kept, d_branch_row, n_batch)
    grad_out_part = jnp.concatenate([grad_out_part, packed_part], axis=1)
    grad_out_part, reduced = tie(grad_out_part, reduced)
    reduced_out = scatter_batch(grad_out_part, n_batch)
    blocks = [
        flip(lax.dynamic_slice_in_dim(reduced, (me ^ bit) * own, own, 0), "seq", bit, n_seq)
        if bit
        else lax.dynamic_slice_in_dim(reduced, me * own, own, 0)
        for bit in range(n_seq)
    ]
    grad_qkv = format_qkv(me.reshape(1), blocks, width, n_seq)
    grad_qkv, *feed_blocks = tie(grad_qkv, *feed_blocks)
    feed = scatter_end(scatter_next(feed_blocks, n_seq)) + down_bias
    layer_out = (middle_own + active * feed).astype(LOW)
    parts_one = scatter_next(blocks_one, n_seq)
    parts_one[0][0], reduced_out = tie(parts_one[0][0], reduced_out)
    d_normed_one = scatter_end(parts_one)
    row_own = tokens.astype(WIDE)
    centre_own, inverse_first = norm_stats(row_own)
    d_input = d_middle + norm_backward(
        d_normed_one, (row_own - centre_own) * inverse_first, inverse_first, gain_one
    )
    grad_out = reduced_out[:, :width]
    small_rows = reduced_out[: n_seq * rows_back, width:].reshape(n_seq, rows_back, EXTRA)
    small_rows = exchange(
        [lax.dynamic_index_in_dim(small_rows, me ^ bit, 0, False) for bit in range(n_seq)], n_seq
    )
    small_out = scatter_end([[block] for block in small_rows]).reshape(-1)
    small_result, at = [], 0
    for size in sizes:
        small_result.append(small_out[at : at + size])
        at += size
    g_one, c_one, g_qvb, g_outb, g_two, c_two, g_upb, g_downb = small_result
    return (
        layer_out[None],
        d_input[None],
        g_one,
        c_one,
        grad_qkv,
        g_qvb,
        grad_out.astype(WIDE),
        g_outb,
        g_two,
        c_two,
        grad_up.astype(WIDE),
        g_upb,
        grad_down.astype(WIDE),
        g_downb,
    )


def solution(mesh):
    vector = P(("seq", "batch"))
    matrix = P(("seq", "batch"), None)
    rows = P("batch", "seq", None)
    return jax.shard_map(
        functools.partial(shards, mesh.shape["seq"], mesh.shape["batch"]),
        mesh=mesh,
        in_specs=(
            rows, rows, P("batch", None), P("batch", "seq"),
            vector, vector, matrix, vector, matrix, vector, vector, vector, matrix, vector, matrix, vector,
        ),
        out_specs=(
            rows, rows, vector, vector, matrix, vector, matrix, vector, vector, vector, matrix, vector, matrix, vector,
        ),
        check_vma=False,
    )
```

```python
import functools

import jax
import jax.numpy as jnp
from jax import lax
from jax.experimental import pallas as pl
from jax.experimental.pallas import tpu as pltpu
from jax.sharding import PartitionSpec as P

HEADS = 32
HEAD_DIM = 64
TILE = 128
PAIR = 2 * HEAD_DIM
Q_BLOCK = 256
FFN_ROWS = 512
EXTRA = 128
EPSILON = 1e-05
GELU_C = 0.7978845608028654
GELU_K = 0.044715
NEGATIVE = -1e30
VMEM_LIMIT = 56 * 1024 * 1024
LOW = jnp.bfloat16
WIDE = jnp.float32


def cost(microseconds):
    return pl.CostEstimate(flops=int(microseconds * 0.4 * 1.15e9), bytes_accessed=1 << 10, transcendentals=0)


def product(left, right):
    return jnp.dot(left, right, preferred_element_type=WIDE)


def product_t(left, right):
    return lax.dot_general(left, right, (((1,), (1,)), ((), ())), preferred_element_type=WIDE)


def product_rows(left, right):
    return lax.dot_general(left, right, (((0,), (0,)), ((), ())), preferred_element_type=WIDE)


def norm_stats(values):
    centre = jnp.mean(values, axis=-1, keepdims=True)
    centred = values - centre
    spread = jnp.mean(centred * centred, axis=-1, keepdims=True)
    return centre, lax.rsqrt(spread + EPSILON)


def norm_backward(upstream, normed, inverse, gain):
    graded = upstream * gain
    first = jnp.mean(graded, axis=-1, keepdims=True)
    second = jnp.mean(graded * normed, axis=-1, keepdims=True)
    return inverse * (graded - first - normed * second)


def flip(values, axis, bit, size):
    return lax.ppermute(values, axis, [(i, i ^ bit) for i in range(size)])


def tie(*values):
    return lax.optimization_barrier(values)


def gather_start(values, n_seq):
    if n_seq != 4:
        return [values] + [flip(values, "seq", bit, n_seq) for bit in range(1, n_seq)]
    return [values, flip(values, "seq", 1, 4), flip(values, "seq", 2, 4)]


def gather_end(held, n_seq):
    if n_seq != 4:
        return held
    values, one, two = held
    half = values.shape[0] // 2
    low = flip(one[:half], "seq", 2, 4)
    high = flip(two[half:], "seq", 1, 4)
    return [values, one, two, jnp.concatenate([low, high], axis=0)]


def exchange(blocks, n_seq):
    return [blocks[0]] + [flip(blocks[bit], "seq", bit, n_seq) for bit in range(1, n_seq)]


def scatter_start(blocks, n_seq):
    if n_seq != 4:
        return exchange(blocks, n_seq)
    own, first, second, then_second, then_first = blocks
    return [own, flip(first, "seq", 1, 4), flip(second, "seq", 2, 4), then_second, then_first]


def scatter_next(blocks, n_seq):
    if n_seq != 4:
        return [[block] for block in blocks]
    own, first, second, then_second, then_first = blocks
    half = own.shape[0] // 2
    then_second = (then_second.astype(WIDE) + first[half:].astype(WIDE)).astype(LOW)
    then_first = (then_first.astype(WIDE) + second[half:].astype(WIDE)).astype(LOW)
    then_second, then_first = flip(then_second, "seq", 2, 4), flip(then_first, "seq", 1, 4)
    return [[own], [first, second], [then_second, then_first]]


def scatter_send(blocks, n_seq):
    return scatter_next(scatter_start(blocks, n_seq), n_seq)


def scatter_end(parts):
    count = parts[0][0].shape[0]
    total = parts[0][0].astype(WIDE)
    for part in parts[1:]:
        rows = count // len(part)
        total = total + jnp.concatenate([piece[:rows] for piece in part], axis=0).astype(WIDE)
    return total


def pair_split(left, n_batch):
    side = lax.axis_index("batch") & 1
    blocks = left.reshape(left.shape[0], n_batch // 2, 2, left.shape[1] // n_batch)
    sent = lax.dynamic_index_in_dim(blocks, 1 - side, 2, False)
    kept = lax.dynamic_index_in_dim(blocks, side, 2, False)
    return sent.reshape(left.shape[0], -1), kept.reshape(left.shape[0], -1)


def rows_kernel(side_ref, left_ref, right_ref, *refs):
    total = product_rows(left_ref[...], right_ref[...])
    if len(refs) == 2:
        total += refs[0][...].astype(WIDE)
    refs[-1][...] = total.astype(LOW)


def rows_product(side, left, right, added, n_batch):
    length, columns = left.shape
    width = right.shape[1]
    count = columns // n_batch
    block = pl.BlockSpec((count, width), lambda k, side: (k, 0))
    return pl.pallas_call(
        rows_kernel,
        grid_spec=pltpu.PrefetchScalarGridSpec(
            num_scalar_prefetch=1,
            grid=(n_batch // 2,),
            in_specs=[
                pl.BlockSpec((length, count), lambda k, side: (0, 2 * k + side[0])),
                pl.BlockSpec((length, width), lambda k, side: (0, 0), pipeline_mode=pl.Buffered(1)),
            ]
            + [block] * len(added),
            out_specs=block,
        ),
        out_shape=jax.ShapeDtypeStruct((columns // 2, width), LOW),
        compiler_params=pltpu.CompilerParams(vmem_limit_bytes=VMEM_LIMIT),
        cost_estimate=cost(9),
        name="rows_product",
    )(side, left, right, *added)


def pair_rows(left, right, n_batch):
    if left.shape[1] // n_batch % 128:
        return pair_product(*pair_split(left, n_batch), right, n_batch)
    side = (lax.axis_index("batch") & 1).reshape(1)
    moved = flip(rows_product(1 - side, left, right, (), n_batch), "batch", 1, n_batch)
    return rows_product(side, left, right, (moved,), n_batch)


def pair_product(sent, kept, right, n_batch):
    moved = flip(product_rows(sent, right).astype(LOW), "batch", 1, n_batch)
    return (product_rows(kept, right) + moved.astype(WIDE)).astype(LOW)


def scatter_batch(total, n_batch):
    groups = [list(range(0, n_batch, 2)), list(range(1, n_batch, 2))]
    return lax.psum_scatter(
        total,
        "batch",
        scatter_dimension=0,
        tiled=True,
        axis_index_groups=groups,
    )


def key_range(q_start, q_count, length):
    low = max(0, (q_start - (length // 2 - 1)) // q_count * q_count)
    return low, q_start + q_count


def block_mask(starts, low, high, q_start, q_count):
    shape = (high - low, q_count)
    key = low + lax.broadcasted_iota(jnp.int32, shape, 0)
    query = q_start + lax.broadcasted_iota(jnp.int32, shape, 1)
    return (key <= query) & (key >= starts)


def load_natural(me, pairs):
    for source, target in pairs:
        for block in range(target.shape[0] // Q_BLOCK):
            at = pl.multiple_of((block ^ me) * Q_BLOCK, Q_BLOCK)
            target[block * Q_BLOCK : (block + 1) * Q_BLOCK, :] = source[pl.ds(at, Q_BLOCK), :]


def attend_kernel(me_ref, q_ref, k_ref, v_ref, start_ref, o_ref, lse_ref, k_own, v_own):
    length = q_ref.shape[0]
    me = me_ref[0]
    load_natural(me, ((k_ref, k_own), (v_ref, v_own)))
    lane = lax.broadcasted_iota(jnp.int32, (1, PAIR), 1)
    row = lax.broadcasted_iota(jnp.int32, (PAIR, 1), 0)
    for q_start in range(0, length, Q_BLOCK):
        low, high = key_range(q_start, Q_BLOCK, length)
        here = slice(q_start, q_start + Q_BLOCK)
        there = pl.ds(pl.multiple_of((q_start // Q_BLOCK ^ me) * Q_BLOCK, Q_BLOCK), Q_BLOCK)
        q, k, v = q_ref[there, :], k_own[low:high, :], v_own[low:high, :]
        allowed = block_mask(start_ref[:, here], low, high, q_start, Q_BLOCK)
        mixed = []
        for head in range(2):
            mine = (lane >= head * HEAD_DIM) & (lane < (head + 1) * HEAD_DIM)
            q_head = jnp.where(mine, q, jnp.zeros_like(q))
            scores = product_t(k, q_head) * HEAD_DIM ** (-0.5)
            scores = jnp.where(allowed, scores, NEGATIVE)
            peak = jnp.max(scores, axis=0, keepdims=True)
            raised = jnp.exp(scores - peak)
            total = jnp.sum(raised, axis=0, keepdims=True)
            probs = (raised / total).astype(LOW)
            mixed.append(product_rows(v, probs))
            lse_ref[0, head : head + 1, here] = peak + jnp.log(total)
        joined = jnp.where(row < HEAD_DIM, mixed[0], mixed[1])
        o_ref[there, :] = joined.T.astype(LOW)


def attend(me, qkv, starts, width):
    length = qkv.shape[0]
    pairs = width // PAIR
    return pl.pallas_call(
        attend_kernel,
        grid_spec=pltpu.PrefetchScalarGridSpec(
            num_scalar_prefetch=1,
            grid=(pairs,),
            in_specs=[
                pl.BlockSpec((length, PAIR), lambda j, me: (0, j)),
                pl.BlockSpec((length, PAIR), lambda j, me: (0, pairs + j)),
                pl.BlockSpec((length, PAIR), lambda j, me: (0, 2 * pairs + j)),
                pl.BlockSpec((1, length), lambda j, me: (0, 0)),
            ],
            out_specs=[
                pl.BlockSpec((length, PAIR), lambda j, me: (0, j)),
                pl.BlockSpec((1, 2, length), lambda j, me: (j, 0, 0)),
            ],
            scratch_shapes=[pltpu.VMEM((length, PAIR), LOW), pltpu.VMEM((length, PAIR), LOW)],
        ),
        out_shape=[
            jax.ShapeDtypeStruct((length, width), LOW),
            jax.ShapeDtypeStruct((pairs, 2, length), WIDE),
        ],
        compiler_params=pltpu.CompilerParams(vmem_limit_bytes=VMEM_LIMIT),
        cost_estimate=cost(20.5),
        name="attend",
    )(me, qkv, qkv, qkv, starts)


def attend_back_kernel(
    me_ref, q_ref, k_ref, v_ref, do_ref, start_ref, lse_ref, out_ref, k_own, v_own, dk_acc, dv_acc
):
    length = q_ref.shape[0]
    width = out_ref.shape[1] // 3
    me = me_ref[0]
    at = pl.program_id(0) * PAIR
    scale = HEAD_DIM ** (-0.5)
    lane = lax.broadcasted_iota(jnp.int32, (1, PAIR), 1)
    row = lax.broadcasted_iota(jnp.int32, (PAIR, 1), 0)
    load_natural(me, ((k_ref, k_own), (v_ref, v_own)))
    dk_acc[...] = jnp.zeros_like(dk_acc)
    dv_acc[...] = jnp.zeros_like(dv_acc)
    for q_start in range(0, length, Q_BLOCK):
        low, high = key_range(q_start, Q_BLOCK, length)
        here = slice(q_start, q_start + Q_BLOCK)
        there = pl.ds(pl.multiple_of((q_start // Q_BLOCK ^ me) * Q_BLOCK, Q_BLOCK), Q_BLOCK)
        q, k, v, do = q_ref[there, :], k_own[low:high, :], v_own[low:high, :], do_ref[there, :]
        allowed = block_mask(start_ref[:, here], low, high, q_start, Q_BLOCK)
        d_query = []
        for head in range(2):
            mine = (lane >= head * HEAD_DIM) & (lane < (head + 1) * HEAD_DIM)
            q_head = jnp.where(mine, q, jnp.zeros_like(q))
            do_head = jnp.where(mine, do, jnp.zeros_like(do))
            scores = product_t(k, q_head) * scale - lse_ref[0, head : head + 1, here]
            probs = jnp.exp(jnp.where(allowed, scores, NEGATIVE))
            d_probs = product_t(v, do_head)
            delta = jnp.sum(probs * d_probs, axis=0, keepdims=True)
            d_scores = (probs * (d_probs - delta)).astype(LOW)
            d_query.append(product_rows(k, d_scores))
            dk_acc[low:high, :] += product(d_scores, q_head)
            dv_acc[low:high, :] += product(probs.astype(LOW), do_head)
        joined = jnp.where(row < HEAD_DIM, d_query[0], d_query[1]) * scale
        out_ref[there, pl.ds(pl.multiple_of(at, PAIR), PAIR)] = joined.T.astype(LOW)
    for q_start in range(0, length, Q_BLOCK):
        here = slice(q_start, q_start + Q_BLOCK)
        there = pl.ds(pl.multiple_of((q_start // Q_BLOCK ^ me) * Q_BLOCK, Q_BLOCK), Q_BLOCK)
        d_key = (dk_acc[here, :] * scale).astype(LOW)
        out_ref[there, pl.ds(pl.multiple_of(width + at, PAIR), PAIR)] = d_key
        d_value = dv_acc[here, :].astype(LOW)
        out_ref[there, pl.ds(pl.multiple_of(2 * width + at, PAIR), PAIR)] = d_value


def attend_back(me, qkv, d_mixed, starts, logsum, width):
    length = qkv.shape[0]
    pairs = width // PAIR
    return pl.pallas_call(
        attend_back_kernel,
        grid_spec=pltpu.PrefetchScalarGridSpec(
            num_scalar_prefetch=1,
            grid=(pairs,),
            in_specs=[
                pl.BlockSpec((length, PAIR), lambda j, me: (0, j)),
                pl.BlockSpec((length, PAIR), lambda j, me: (0, pairs + j)),
                pl.BlockSpec((length, PAIR), lambda j, me: (0, 2 * pairs + j)),
                pl.BlockSpec((length, PAIR), lambda j, me: (0, j)),
                pl.BlockSpec((1, length), lambda j, me: (0, 0)),
                pl.BlockSpec((1, 2, length), lambda j, me: (j, 0, 0)),
            ],
            out_specs=pl.BlockSpec((length, 3 * width), lambda j, me: (0, 0)),
            scratch_shapes=[
                pltpu.VMEM((length, PAIR), LOW),
                pltpu.VMEM((length, PAIR), LOW),
                pltpu.VMEM((length, PAIR), WIDE),
                pltpu.VMEM((length, PAIR), WIDE),
            ],
        ),
        out_shape=jax.ShapeDtypeStruct((length, 3 * width), LOW),
        compiler_params=pltpu.CompilerParams(vmem_limit_bytes=VMEM_LIMIT),
        cost_estimate=cost(23.4),
        name="attend_back",
    )(me, qkv, qkv, qkv, d_mixed, starts, logsum)


def out_norm_kernel(n_seq, *refs):
    o_refs = refs[:n_seq]
    w_ref, row_ref, active_ref, bias_ref, gain_ref, shift_ref = refs[n_seq : n_seq + 6]
    low_ref, middle_ref, normed_ref, inverse_ref = refs[n_seq + 6 :]
    depth = o_refs[0].shape[1]
    branch = product(o_refs[0][...], w_ref[:depth, :])
    for block in range(1, n_seq):
        branch += product(o_refs[block][...], w_ref[block * depth : (block + 1) * depth, :])
    middle = row_ref[...].astype(WIDE) + active_ref[...] * (branch + bias_ref[...])
    centre, inverse = norm_stats(middle)
    normed = (middle - centre) * inverse
    low_ref[...] = (normed * gain_ref[...] + shift_ref[...]).astype(LOW)

    @pl.when(pl.program_id(0) == 0)
    def _():
        middle_ref[...] = middle
        normed_ref[...] = normed
        inverse_ref[...] = inverse


def out_norm(mixed_all, out_full, row_low, active_row, bias, gain, shift, n_seq):
    length, width = row_low.shape
    count = length // n_seq
    depth = width // n_seq

    def mixed_spec(bit):
        return pl.BlockSpec((count, depth), lambda k: (k ^ bit, 0))

    vector = pl.BlockSpec((1, width), lambda k: (0, 0))
    block = pl.BlockSpec((count, width), lambda k: (k, 0))
    first = pl.BlockSpec((count, width), lambda k: (0, 0))
    return pl.pallas_call(
        functools.partial(out_norm_kernel, n_seq),
        grid=(n_seq,),
        in_specs=[mixed_spec(bit) for bit in range(n_seq)]
        + [
            pl.BlockSpec((width, width), lambda k: (0, 0)),
            block,
            pl.BlockSpec((count, 1), lambda k: (k, 0)),
            vector,
            vector,
            vector,
        ],
        out_specs=[block, first, first, pl.BlockSpec((count, 1), lambda k: (0, 0))],
        out_shape=[
            jax.ShapeDtypeStruct((length, width), LOW),
            jax.ShapeDtypeStruct((count, width), WIDE),
            jax.ShapeDtypeStruct((count, width), WIDE),
            jax.ShapeDtypeStruct((count, 1), WIDE),
        ],
        compiler_params=pltpu.CompilerParams(vmem_limit_bytes=VMEM_LIMIT),
        cost_estimate=cost(19.4),
        name="out_norm",
    )(
        *mixed_all,
        out_full,
        row_low,
        active_row,
        bias.reshape(1, width),
        gain.reshape(1, width),
        shift.reshape(1, width),
    )


def assemble_kernel(me_ref, joined_ref, full_ref, extra_ref):
    own = joined_ref.shape[2]
    width = full_ref.shape[1]
    for member in range(joined_ref.shape[0]):
        rows = slice(member * own, (member + 1) * own)
        full_ref[rows, :] = joined_ref[member, 0, :, :width]
        extra_ref[rows, :] = joined_ref[member, 0, :, width:]


def assemble(me, joined, width):
    n_batch, n_seq, own, columns = joined.shape
    count = n_batch * own
    return pl.pallas_call(
        assemble_kernel,
        grid_spec=pltpu.PrefetchScalarGridSpec(
            num_scalar_prefetch=1,
            grid=(n_seq,),
            in_specs=[
                pl.BlockSpec((n_batch, 1, own, columns), lambda j, me: (0, j ^ me[0], 0, 0)),
            ],
            out_specs=[
                pl.BlockSpec((count, width), lambda j, me: (j, 0)),
                pl.BlockSpec((count, EXTRA), lambda j, me: (j, 0)),
            ],
        ),
        out_shape=[
            jax.ShapeDtypeStruct((n_seq * count, width), LOW),
            jax.ShapeDtypeStruct((n_seq * count, EXTRA), LOW),
        ],
        compiler_params=pltpu.CompilerParams(vmem_limit_bytes=VMEM_LIMIT),
        cost_estimate=cost(6.2),
        name="assemble",
    )(me, joined)


def ffn_up_kernel(n_ref, w_ref, bias_ref, hidden_ref, slope_ref):
    step = 512
    for at in range(0, w_ref.shape[0], step):
        here = slice(at, at + step)
        before = product_t(n_ref[...], w_ref[here, :]) + bias_ref[:, here]
        square = before * before
        tangent = jnp.tanh(before * (GELU_C + GELU_C * GELU_K * square))
        half = 0.5 + 0.5 * tangent
        hidden = before * half
        hidden_ref[:, here] = hidden.astype(LOW)
        slope_ref[:, here] = half + hidden * (1.0 - tangent) * (
            GELU_C + 3.0 * GELU_C * GELU_K * square
        )


def ffn_up(normed, w_up, bias):
    length, width = normed.shape
    hidden = w_up.shape[0]
    return pl.pallas_call(
        ffn_up_kernel,
        grid=(length // FFN_ROWS,),
        in_specs=[
            pl.BlockSpec((FFN_ROWS, width), lambda k: (k, 0)),
            pl.BlockSpec((hidden, width), lambda k: (0, 0), pipeline_mode=pl.Buffered(1)),
            pl.BlockSpec((1, hidden), lambda k: (0, 0)),
        ],
        out_specs=[
            pl.BlockSpec((FFN_ROWS, hidden), lambda k: (k, 0)),
            pl.BlockSpec((FFN_ROWS, hidden), lambda k: (k, 0)),
        ],
        out_shape=[
            jax.ShapeDtypeStruct((length, hidden), LOW),
            jax.ShapeDtypeStruct((length, hidden), WIDE),
        ],
        compiler_params=pltpu.CompilerParams(vmem_limit_bytes=VMEM_LIMIT),
        cost_estimate=cost(19.6),
        name="ffn_up",
    )(normed, w_up, bias.reshape(1, hidden))


def split_sizes(count, n_seq):
    return [count] * n_seq if n_seq != 4 else [count, count, count, count // 2, count // 2]


def split_specs(count, width, n_seq):
    return [pl.BlockSpec((size, width), lambda k: (0, 0)) for size in split_sizes(count, n_seq)]


def split_shapes(count, width, n_seq):
    return [jax.ShapeDtypeStruct((size, width), LOW) for size in split_sizes(count, n_seq)]


def split_store(index, values, outs, n_seq):
    half = values.shape[0] // 2
    if n_seq != 4:
        places = [[(outs[bit], 0, slice(None))] for bit in range(n_seq)]
    else:
        own, first, second, then_second, then_first = outs
        upper, lower = slice(0, half), slice(half, 2 * half)
        places = [
            [(own, 0, slice(None))],
            [(first, 0, upper), (then_first, 0, lower)],
            [(then_second, 0, upper), (second, 0, lower)],
            [(first, half, upper), (second, half, lower)],
        ]
    for bit, targets in enumerate(places):

        @pl.when(index == bit)
        def _():
            for target, at, rows in targets:
                piece = values[rows]
                target[at : at + piece.shape[0], :] = piece


def ffn_back_kernel(n_seq, grad_ref, slope_ref, down_ref, up_ref, d_before_ref, sum_ref, *refs):
    outs, (down, up, sems) = refs[:-3], refs[-3:]
    index = pl.program_id(0)
    load_down = pltpu.make_async_copy(down_ref, down, sems.at[0])
    load_up = pltpu.make_async_copy(up_ref, up, sems.at[1])

    @pl.when(index == 0)
    def _():
        load_down.start()
        load_up.start()
        sum_ref[...] = jnp.zeros_like(sum_ref)
        load_down.wait()

    step = 512
    for at in range(0, down.shape[0], step):
        here = slice(at, at + step)
        d_hidden = product_t(grad_ref[...], down[here, :])
        d_before = (d_hidden * slope_ref[:, here]).astype(LOW)
        d_before_ref[:, here] = d_before
        sum_ref[:, here] += jnp.sum(d_before.astype(WIDE), axis=0, keepdims=True)

    @pl.when(index == 0)
    def _():
        load_up.wait()

    d_normed = product(d_before_ref[...], up[...]).astype(LOW)
    split_store(index, d_normed, outs, n_seq)


def ffn_back(grad_row, slope, w_down, w_up, n_seq):
    length, width = grad_row.shape
    hidden = w_up.shape[0]
    count = length // n_seq
    return pl.pallas_call(
        functools.partial(ffn_back_kernel, n_seq),
        grid=(n_seq,),
        in_specs=[
            pl.BlockSpec((count, width), lambda k: (k, 0)),
            pl.BlockSpec((count, hidden), lambda k: (k, 0)),
            pl.BlockSpec(memory_space=pl.ANY),
            pl.BlockSpec(memory_space=pl.ANY),
        ],
        out_specs=[
            pl.BlockSpec((count, hidden), lambda k: (k, 0)),
            pl.BlockSpec((1, hidden), lambda k: (0, 0)),
        ]
        + split_specs(count, width, n_seq),
        out_shape=[
            jax.ShapeDtypeStruct((length, hidden), LOW),
            jax.ShapeDtypeStruct((1, hidden), WIDE),
        ]
        + split_shapes(count, width, n_seq),
        scratch_shapes=[
            pltpu.VMEM((hidden, width), LOW),
            pltpu.VMEM((hidden, width), LOW),
            pltpu.SemaphoreType.DMA((2,)),
        ],
        compiler_params=pltpu.CompilerParams(vmem_limit_bytes=VMEM_LIMIT),
        cost_estimate=cost(28),
        name="ffn_back",
    )(grad_row, slope, w_down, w_up)


def feed_kernel(n_seq, hidden_ref, down_ref, *outs):
    values = product(hidden_ref[...], down_ref[...]).astype(LOW)
    split_store(pl.program_id(0), values, outs, n_seq)


def feed_down(hidden_low, w_down, n_seq):
    length, hidden = hidden_low.shape
    width = w_down.shape[1]
    count = length // n_seq
    return pl.pallas_call(
        functools.partial(feed_kernel, n_seq),
        grid=(n_seq,),
        in_specs=[
            pl.BlockSpec((count, hidden), lambda k: (k, 0)),
            pl.BlockSpec((hidden, width), lambda k: (0, 0), pipeline_mode=pl.Buffered(1)),
        ],
        out_specs=split_specs(count, width, n_seq),
        out_shape=split_shapes(count, width, n_seq),
        compiler_params=pltpu.CompilerParams(vmem_limit_bytes=VMEM_LIMIT),
        cost_estimate=cost(15.6),
        name="feed_down",
    )(hidden_low, w_down)


def qkv_back_kernel(n_seq, grad_ref, w_ref, row_ref, sums_ref, bias_ref, *outs):
    index = pl.program_id(0)

    @pl.when(index == 0)
    def _():
        sums_ref[...] = jnp.zeros_like(sums_ref)
        bias_ref[...] = jnp.zeros_like(bias_ref)

    d_normed = product_t(grad_ref[...], w_ref[...])
    row = row_ref[...].astype(WIDE)
    centre, inverse = norm_stats(row)
    normed = (row - centre) * inverse
    sums_ref[0:1, :] += jnp.sum(d_normed * normed, axis=0, keepdims=True)
    sums_ref[1:2, :] += jnp.sum(d_normed, axis=0, keepdims=True)
    bias_ref[0:1, :] += jnp.sum(grad_ref[...].astype(WIDE), axis=0, keepdims=True)
    split_store(index, d_normed.astype(LOW), outs, n_seq)


def qkv_back(d_qkv, qkv_full, row_low, n_seq):
    length, width = row_low.shape
    columns = d_qkv.shape[1]
    count = length // n_seq
    return pl.pallas_call(
        functools.partial(qkv_back_kernel, n_seq),
        grid=(n_seq,),
        in_specs=[
            pl.BlockSpec((count, columns), lambda k: (k, 0)),
            pl.BlockSpec((width, columns), lambda k: (0, 0), pipeline_mode=pl.Buffered(1)),
            pl.BlockSpec((count, width), lambda k: (k, 0)),
        ],
        out_specs=[
            pl.BlockSpec((8, width), lambda k: (0, 0)),
            pl.BlockSpec((8, columns), lambda k: (0, 0)),
        ]
        + split_specs(count, width, n_seq),
        out_shape=[
            jax.ShapeDtypeStruct((8, width), WIDE),
            jax.ShapeDtypeStruct((8, columns), WIDE),
        ]
        + split_shapes(count, width, n_seq),
        compiler_params=pltpu.CompilerParams(vmem_limit_bytes=VMEM_LIMIT),
        cost_estimate=cost(15.3),
        name="qkv_back",
    )(d_qkv, qkv_full, row_low)


def norm_back_kernel(pieces, *refs):
    n_parts = sum(pieces)
    parts, at = [], 0
    for number in pieces:
        parts.append(refs[at : at + number])
        at += number
    cot_ref, normed_ref, inverse_ref, active_ref, gain_ref, w_ref = refs[n_parts : n_parts + 6]
    d_middle_ref, d_branch_ref, d_mixed_ref, sums_ref = refs[n_parts + 6 :]

    @pl.when(pl.program_id(0) == 0)
    def _():
        upstream = parts[0][0][...].astype(WIDE)
        for part in parts[1:]:
            upstream += jnp.concatenate([piece[...] for piece in part], axis=0).astype(WIDE)
        normed = normed_ref[...]
        d_middle = cot_ref[...].astype(WIDE) + norm_backward(
            upstream, normed, inverse_ref[...], gain_ref[...]
        )
        d_middle_ref[...] = d_middle
        d_branch = (d_middle * active_ref[...]).astype(LOW)
        d_branch_ref[...] = d_branch
        sums_ref[...] = jnp.zeros_like(sums_ref)
        sums_ref[0:1, :] = jnp.sum(upstream * normed, axis=0, keepdims=True)
        sums_ref[1:2, :] = jnp.sum(upstream, axis=0, keepdims=True)
        sums_ref[2:3, :] = jnp.sum(d_branch.astype(WIDE), axis=0, keepdims=True)

    d_mixed_ref[0] = product_t(d_branch_ref[...], w_ref[...]).astype(LOW)


def norm_back(parts, cotangent, normed, inverse, active, gain, out_full, n_seq):
    count, width = cotangent.shape
    depth = width // n_seq
    block = pl.BlockSpec((count, width), lambda j: (0, 0))
    column = pl.BlockSpec((count, 1), lambda j: (0, 0))
    return pl.pallas_call(
        functools.partial(norm_back_kernel, [len(part) for part in parts]),
        grid=(n_seq,),
        in_specs=[
            pl.BlockSpec((count // len(part), width), lambda j: (0, 0)) for part in parts for piece in part
        ]
        + [block, block]
        + [
            column,
            column,
            pl.BlockSpec((1, width), lambda j: (0, 0)),
            pl.BlockSpec((depth, width), lambda j: (j, 0)),
        ],
        out_specs=[
            block,
            block,
            pl.BlockSpec((1, count, depth), lambda j: (j, 0, 0)),
            pl.BlockSpec((8, width), lambda j: (0, 0)),
        ],
        out_shape=[
            jax.ShapeDtypeStruct((count, width), WIDE),
            jax.ShapeDtypeStruct((count, width), LOW),
            jax.ShapeDtypeStruct((n_seq, count, depth), LOW),
            jax.ShapeDtypeStruct((8, width), WIDE),
        ],
        compiler_params=pltpu.CompilerParams(vmem_limit_bytes=VMEM_LIMIT),
        cost_estimate=cost(11),
        name="norm_back",
    )(
        *[piece for part in parts for piece in part],
        cotangent,
        normed,
        inverse,
        active,
        gain.reshape(1, width),
        out_full,
    )


def format_kernel(n_seq, me_ref, *refs):
    out_ref = refs[n_seq]
    width = out_ref.shape[1] // 3
    count = width // n_seq
    for block in range(n_seq):
        ref = refs[block]
        for kind in range(3):
            at = kind * width + (me_ref[0] ^ block) * count
            at = pl.multiple_of(at, count)
            out_ref[:, pl.ds(at, count)] = ref[:, kind * count : (kind + 1) * count].astype(WIDE)


def format_qkv(me, blocks, width, n_seq):
    own = blocks[0].shape[0]
    return pl.pallas_call(
        functools.partial(format_kernel, n_seq),
        grid_spec=pltpu.PrefetchScalarGridSpec(
            num_scalar_prefetch=1,
            grid=(1,),
            in_specs=[pl.BlockSpec(blocks[0].shape, lambda i, me: (0, 0))] * n_seq,
            out_specs=pl.BlockSpec((own, 3 * width), lambda i, me: (0, 0)),
        ),
        out_shape=jax.ShapeDtypeStruct((own, 3 * width), WIDE),
        compiler_params=pltpu.CompilerParams(vmem_limit_bytes=VMEM_LIMIT),
        cost_estimate=cost(2.5),
        name="format_qkv",
    )(me, *blocks)


def gather_shared(values, n_seq, n_batch):
    half = values.shape[0] // 2
    side = lax.axis_index("batch") & 1
    mine = lax.dynamic_slice_in_dim(values, side * half, half, 0)
    held = gather_end(gather_start(mine, n_seq), n_seq)[1:]
    other = [flip(block, "batch", 1, n_batch) for block in held]
    blocks = [values]
    for mine, theirs in zip(held, other):
        blocks.append(jnp.where(side == 0, mine, theirs))
        blocks.append(jnp.where(side == 0, theirs, mine))
    return blocks


def shards(
    n_seq,
    n_batch,
    tokens,
    cotangent,
    segment_ids,
    exit_mask,
    ln1_gain,
    ln1_bias,
    w_qkv,
    b_qv,
    w_out,
    b_out,
    ln2_gain,
    ln2_bias,
    w_up,
    b_up,
    w_down,
    b_down,
):
    _, local_len, width = tokens.shape
    length = n_seq * local_len
    own = w_qkv.shape[0]
    head_width = width // n_seq
    n_all = n_seq * n_batch
    me = lax.axis_index("seq")
    tokens = tokens.reshape(local_len, width)
    cotangent = cotangent.reshape(local_len, width)

    small_parts = (ln1_gain, ln1_bias, b_qv, b_out, ln2_gain, ln2_bias, b_up, b_down)
    sizes = [part.shape[0] for part in small_parts]
    n_small = sum(sizes)
    tiles = exit_mask.shape[1]
    part_width = 3 * head_width
    small = jnp.concatenate(small_parts + (exit_mask.reshape(-1).astype(LOW),))
    lanes = -(-small.shape[0] // own)
    small = jnp.pad(small, (0, own * lanes - small.shape[0])).reshape(own, lanes)
    small = jnp.pad(small, ((0, 0), (0, EXTRA - lanes)))

    by_head = w_qkv.reshape(own, 3, n_seq, head_width).transpose(2, 0, 1, 3)
    by_head = by_head.reshape(n_seq, own, part_width)
    moved = exchange(
        [
            jnp.concatenate([lax.dynamic_index_in_dim(by_head, me ^ bit, 0, False), small], axis=1)
            for bit in range(n_seq)
        ],
        n_seq,
    )
    held_row = gather_start(tokens, n_seq)
    tied = tie(*moved, *held_row)
    moved, held_row = list(tied[:n_seq]), list(tied[n_seq:])
    moved = jnp.concatenate(moved, axis=0).reshape(n_seq, own, part_width + EXTRA)
    out_part = lax.all_gather(w_out, "batch", axis=0, tiled=True)
    joined = lax.all_gather(moved.reshape(n_seq * own, part_width + EXTRA), "batch", axis=0)
    up_all = lax.all_gather(w_up, "batch", axis=0, tiled=True)
    down_all = lax.all_gather(w_down, "batch", axis=0, tiled=True)
    hidden_count = up_all.shape[0]

    def unpack(extra):
        return extra[..., :lanes].reshape(extra.shape[:-2] + (own * lanes,))

    mask_row = unpack(moved[..., part_width:])[:, n_small : n_small + tiles]
    active_row = jnp.repeat(mask_row.reshape(-1), TILE).astype(WIDE).reshape(length, 1)
    joined = joined.reshape(n_batch, n_seq, own, part_width + EXTRA)
    qkv_full, small_all = assemble(me.reshape(1), joined, part_width)
    small_all = unpack(small_all.reshape(n_seq, n_batch, own, EXTRA)).astype(WIDE)
    params, at = [], 0
    for size in sizes:
        params.append(small_all[:, :, at : at + size].reshape(-1))
        at += size
    gain_one, bias_one, qv_bias, out_bias, gain_two, bias_two, up_bias_all, down_bias = params
    up_bias = lax.dynamic_slice_in_dim(up_bias_all, me * hidden_count, hidden_count)

    *held_row, out_part = tie(*gather_end(held_row, n_seq), out_part)
    row_low = jnp.concatenate(held_row, axis=0)
    out_full = jnp.concatenate(gather_shared(out_part, n_seq, n_batch), axis=0)
    active = jnp.repeat(exit_mask.reshape(-1), TILE).astype(WIDE).reshape(local_len, 1)
    grad_low = (cotangent.astype(WIDE) * active).astype(LOW)
    row_low, out_full, grad_low = tie(row_low, out_full, grad_low)
    held_grad = gather_start(grad_low, n_seq)
    row = row_low.astype(WIDE)
    centre_one, inverse_one = norm_stats(row)
    normed_one = (row - centre_one) * inverse_one
    normed_low = (normed_one * gain_one + bias_one).astype(LOW)
    normed_low, *held_grad = tie(normed_low, *held_grad)
    own_q = lax.dynamic_slice_in_dim(qv_bias, me * head_width, head_width)
    own_v = lax.dynamic_slice_in_dim(qv_bias, width + me * head_width, head_width)
    own_bias = jnp.concatenate([own_q, jnp.zeros_like(own_q), own_v])
    qkv = (product(normed_low, qkv_full) + own_bias).astype(LOW)
    qkv, *held_grad = tie(qkv, *gather_end(held_grad, n_seq))
    grad_row = jnp.concatenate(held_grad, axis=0)
    segment_row = segment_ids.reshape(length)
    starts = jnp.sum(
        (segment_row[None, :] < segment_row[:, None]).astype(jnp.int32), axis=1
    ).reshape(1, length)
    mixed, logsum = attend(me.reshape(1), qkv, starts, head_width)
    mixed_all = gather_end(gather_start(mixed, n_seq), n_seq)
    side = lax.axis_index("batch") & 1
    normed_halves = normed_low.reshape(length, n_seq, n_batch // 2, 2, own).transpose(3, 0, 2, 1, 4)
    normed_halves = normed_halves.reshape(2, length, width // 2)
    normed_sent = lax.dynamic_index_in_dim(normed_halves, 1 - side, 0, False)
    normed_kept = lax.dynamic_index_in_dim(normed_halves, side, 0, False)
    mixed_sent, mixed_kept = pair_split(mixed, n_batch)
    normed_two_low, middle_own, normed_own, inverse_own = out_norm(
        mixed_all, out_full, row_low, active_row, out_bias, gain_two, bias_two, n_seq
    )

    hidden_low, slope = ffn_up(normed_two_low, up_all, up_bias)
    grad_down_part = pair_rows(hidden_low, grad_row, n_batch)
    grad_down_part, down_all, normed_sent, normed_kept, mixed_sent, mixed_kept = tie(
        grad_down_part, down_all, normed_sent, normed_kept, mixed_sent, mixed_kept
    )
    grad_down = scatter_batch(grad_down_part, n_batch)
    d_before, grad_upb, *blocks = ffn_back(grad_row, slope, down_all, up_all, n_seq)
    parts = scatter_send(blocks, n_seq)
    grad_up_part = pair_rows(d_before, normed_two_low, n_batch)
    feed_blocks = feed_down(hidden_low, down_all, n_seq)
    parts[0][0], grad_up_part, *feed_blocks = tie(parts[0][0], grad_up_part, *feed_blocks)
    grad_up = scatter_batch(grad_up_part, n_batch)
    grad_downb = jnp.sum(grad_low.astype(WIDE), axis=0)

    d_middle, d_branch, d_mixed, sums = norm_back(
        parts, cotangent, normed_own, inverse_own, active, gain_two, out_full, n_seq
    )
    d_mixed = jnp.concatenate(exchange([d_mixed[bit] for bit in range(n_seq)], n_seq), axis=0)
    d_mixed, d_branch = tie(d_mixed, d_branch)
    held_branch = gather_start(d_branch, n_seq)
    d_qkv = attend_back(me.reshape(1), qkv, d_mixed, starts, logsum, head_width)
    tied = tie(d_qkv, *held_branch, *feed_blocks)
    d_qkv, held_branch, feed_blocks = tied[0], tied[1 : len(held_branch) + 1], tied[len(held_branch) + 1 :]
    d_branch_row = jnp.concatenate(gather_end(held_branch, n_seq), axis=0)

    grad_qkv_part = pair_product(normed_sent, normed_kept, d_qkv, n_batch)
    grad_qkv_part, grad_up, grad_down = tie(grad_qkv_part, grad_up, grad_down)
    reduced = scatter_batch(grad_qkv_part, n_batch)

    sums_one, d_bias, *blocks_one = qkv_back(d_qkv, qkv_full, row_low, n_seq)
    d_bias = d_bias[0]
    tied = tie(*scatter_start(blocks_one, n_seq), *feed_blocks)
    blocks_one, feed_blocks = tied[: len(blocks_one)], scatter_start(tied[len(blocks_one) :], n_seq)

    def place(values, total):
        return lax.dynamic_update_slice_in_dim(
            jnp.zeros((total,), WIDE), values, me * values.shape[0], 0
        )

    grad_qvb = jnp.concatenate(
        [place(d_bias[:head_width], width), place(d_bias[2 * head_width :], width)]
    )
    small_grads = (
        sums_one[0],
        sums_one[1],
        grad_qvb,
        sums[2],
        sums[0],
        sums[1],
        place(grad_upb.reshape(-1), n_seq * hidden_count),
        grad_downb,
    )
    packed = jnp.concatenate([g.reshape(n_seq, n_batch, -1) for g in small_grads], axis=2)
    rows_back = -(-n_small // EXTRA)
    packed = jnp.pad(packed, ((0, 0), (0, 0), (0, rows_back * EXTRA - n_small)))
    packed = packed.reshape(n_seq, n_batch, rows_back, EXTRA).transpose(1, 0, 2, 3).astype(LOW)
    packed = packed.reshape(n_batch // 2, 2, n_seq * rows_back, EXTRA)
    packed = jnp.pad(packed, ((0, 0), (0, 0), (0, own - n_seq * rows_back), (0, 0)))
    packed_sent = lax.dynamic_index_in_dim(packed, 1 - side, 1, False).reshape(-1, EXTRA)
    packed_kept = lax.dynamic_index_in_dim(packed, side, 1, False).reshape(-1, EXTRA)
    packed_part = packed_kept + flip(packed_sent, "batch", 1, n_batch)
    grad_out_part = pair_product(mixed_sent, mixed_kept, d_branch_row, n_batch)
    grad_out_part = jnp.concatenate([grad_out_part, packed_part], axis=1)
    grad_up, grad_down = grad_up.astype(WIDE), grad_down.astype(WIDE)
    grad_out_part, grad_up, grad_down = tie(grad_out_part, grad_up, grad_down)
    grad_out_part, reduced = tie(grad_out_part, reduced)
    reduced_out = scatter_batch(grad_out_part, n_batch)
    blocks = [
        flip(lax.dynamic_slice_in_dim(reduced, (me ^ bit) * own, own, 0), "seq", bit, n_seq)
        if bit
        else lax.dynamic_slice_in_dim(reduced, me * own, own, 0)
        for bit in range(n_seq)
    ]
    grad_qkv = format_qkv(me.reshape(1), blocks, width, n_seq)
    grad_qkv, *feed_blocks = tie(grad_qkv, *feed_blocks)
    feed = scatter_end(scatter_next(feed_blocks, n_seq)) + down_bias
    layer_out = (middle_own + active * feed).astype(LOW)
    parts_one = scatter_next(blocks_one, n_seq)
    parts_one[0][0], grad_qkv = tie(parts_one[0][0], grad_qkv)
    d_normed_one = scatter_end(parts_one)
    row_own = tokens.astype(WIDE)
    centre_own, inverse_first = norm_stats(row_own)
    d_input = d_middle + norm_backward(
        d_normed_one, (row_own - centre_own) * inverse_first, inverse_first, gain_one
    )
    grad_out = reduced_out[:, :width]
    small_rows = reduced_out[: n_seq * rows_back, width:].reshape(n_seq, rows_back, EXTRA)
    small_rows = exchange(
        [lax.dynamic_index_in_dim(small_rows, me ^ bit, 0, False) for bit in range(n_seq)], n_seq
    )
    small_out = scatter_end([[block] for block in small_rows]).reshape(-1)
    small_result, at = [], 0
    for size in sizes:
        small_result.append(small_out[at : at + size])
        at += size
    g_one, c_one, g_qvb, g_outb, g_two, c_two, g_upb, g_downb = small_result
    return (
        layer_out[None],
        d_input[None],
        g_one,
        c_one,
        grad_qkv,
        g_qvb,
        grad_out.astype(WIDE),
        g_outb,
        g_two,
        c_two,
        grad_up,
        g_upb,
        grad_down,
        g_downb,
    )


def solution(mesh):
    vector = P(("seq", "batch"))
    matrix = P(("seq", "batch"), None)
    rows = P("batch", "seq", None)
    return jax.shard_map(
        functools.partial(shards, mesh.shape["seq"], mesh.shape["batch"]),
        mesh=mesh,
        in_specs=(
            rows, rows, P("batch", None), P("batch", "seq"),
            vector, vector, matrix, vector, matrix, vector, vector, vector, matrix, vector, matrix, vector,
        ),
        out_specs=(
            rows, rows, vector, vector, matrix, vector, matrix, vector, vector, vector, matrix, vector, matrix, vector,
        ),
        check_vma=False,
    )
```
